32 devices in a mesh: mode: 16 (over z, x, core), node: 2 (over y).
Axes of the slice: x: 2, y: 2, z: 4, core: 2. Of those that a mesh axis runs over, the one named last changes fastest.
Arguments:
- panels: bfloat16 [2, 2048, 4096], P(None, 'node', 'mode'), may hold values from -60 to 60, as said below
- shapes: bfloat16 [8192, 4096], P('mode'), may hold values from -0.09375 to 0.09375
- harmonic: int32 [2048], P('node'), may hold values from 1 to 4095, as said below
- connect: int32 [4096, 8], P(('mode', 'node')), may hold values from 0 to 8191, as said below
- recovery: float32 [4096, 8], P(('mode', 'node')), may hold values from -3 to 3
Outputs:
- stress: float32 [4096, 512], P(('mode', 'node'))
- moments: float32 [4, 8192], P(None, ('mode', 'node'))
The draws below stay inside these ranges and needn't reach their ends.
Inputs may be any that keep to these rules, and one draw needn't show every extreme that they name: `harmonic`: harmonic numbers are distinct and increasing. `connect`: the 128 elements of block b refer only to rows of group b // 2, that is rows (b // 2) * 512 to (b // 2 + 1) * 512 - 1. Split a group's rows into 2 blocks of 256 rows: one element block refers to at most 64 distinct rows of any one such block, and in every group one element block refers to exactly 64 rows of each of them. `panels`: modal coordinates stay in the range.
All inputs are finite; a program needn't handle non-finite values.
Results may differ from the reference program's by a relative error of at most 0.0029.
Values may be sent and summed in bfloat16 or wider, within the bound.
No kernel may reach another device: no remote copies, remote signals or barrier semaphores. Data moves between devices by JAX's collectives and lax.ppermute only.
A program may use at most 64 MiB of HBM per device.

```python
import math
import jax
import jax.numpy as jnp
from jax import lax

M = 4096
F = 2048
STEPS = 512
HARM = 4096
ROWS_MODE = 512
CORNERS = 8
ELEM_DEV = 128
PEERS = 2
BLOCKS = 32
CAP = 64
NDOF = 8192
ELEMS = 4096
N_MODE = 16


def draw_panels(key, part):
    key_main, key_freq, key_mode = jax.random.split(key, 3)
    base_draw = jax.random.normal(key_main, (2, F, M), jnp.float32)
    lowest, highest = (0.3, 3.0)
    freq_scale = jnp.exp(jax.random.uniform(key_freq, (1, F, 1), jnp.float32, math.log(lowest), math.log(highest)))
    mode_scale = jnp.exp(jax.random.uniform(key_mode, (1, 1, M), jnp.float32, math.log(lowest), math.log(highest)))
    return jnp.clip(base_draw * freq_scale * mode_scale, -60.0, 60.0).astype(jnp.bfloat16)


def draw_harmonic(key, part):
    middle = jax.random.permutation(key, HARM - 3)[:F - 2].astype(jnp.int32) + 2
    ends = jnp.array([1, HARM - 1], dtype=jnp.int32)
    return jnp.sort(jnp.concatenate([ends, middle]))


def edge_first(single, rows_dev):
    inner = jax.random.permutation(single, rows_dev - 2).astype(jnp.int32) + 1
    ends = jnp.array([0, rows_dev - 1], dtype=jnp.int32)
    return jnp.concatenate([ends, inner])


def draw_connect(key, part):
    rows_dev = ROWS_MODE // PEERS
    ref_count = ELEM_DEV * CORNERS
    key_first, key_second, key_full, key_perm, key_fill, key_shuffle = jax.random.split(key, 6)
    first_draw = jax.random.randint(key_first, (BLOCKS, PEERS), 0, CAP)
    second_draw = jax.random.randint(key_second, (BLOCKS, PEERS), 0, CAP + 1)
    counts = 1 + first_draw * second_draw // CAP
    full_node = jax.random.randint(key_full, (BLOCKS // PEERS,), 0, PEERS)
    is_full = jnp.arange(BLOCKS) % PEERS == jnp.repeat(full_node, PEERS)
    counts = jnp.where(is_full[:, None], CAP, counts)
    perm_keys = jax.random.split(key_perm, BLOCKS * PEERS)
    row_perms = jax.vmap(lambda single: edge_first(single, rows_dev))(perm_keys)
    row_perms = row_perms.reshape(BLOCKS, PEERS * rows_dev).astype(jnp.int32)
    slot_ids = jnp.arange(CAP)
    valid_pair = (slot_ids[None, None, :] < counts[:, :, None]).reshape(BLOCKS, PEERS * CAP)
    pair_ids = jnp.arange(PEERS * CAP, dtype=jnp.int32)
    ranking = jnp.argsort(jnp.where(valid_pair, 0, PEERS * CAP) + pair_ids[None, :], axis=1)
    valid_count = jnp.sum(valid_pair.astype(jnp.int32), axis=1)
    positions = jnp.arange(ref_count, dtype=jnp.int32)
    extra_pick = jax.random.randint(key_fill, (BLOCKS, ref_count), 0, valid_count[:, None])
    chosen = jnp.where(positions[None, :] < valid_count[:, None], positions[None, :], extra_pick)
    chosen = jnp.take_along_axis(ranking, chosen, axis=1)
    shuffle = jax.vmap(lambda single: jax.random.permutation(single, ref_count))(jax.random.split(key_shuffle, BLOCKS))
    chosen = jnp.take_along_axis(chosen, shuffle, axis=1)
    sources = chosen // CAP
    within = jnp.take_along_axis(row_perms, sources * rows_dev + chosen % CAP, axis=1)
    group_ids = jnp.arange(BLOCKS, dtype=jnp.int32)[:, None] // PEERS
    row_ids = group_ids * ROWS_MODE + sources * rows_dev + within
    return row_ids.reshape(BLOCKS * ELEM_DEV, CORNERS).astype(jnp.int32)


def steps_of(stream_key, extent, pieces, smallest, top_value):
    def one(position, blocks):
        heights = jax.random.uniform(jax.random.fold_in(jax.random.fold_in(stream_key, 6), position), (blocks,), jnp.float32, smallest / len(pieces), top_value / len(pieces))
        return jnp.repeat(jnp.exp(heights), extent[position] // blocks).reshape((-1,) + (1,) * (len(extent) - position - 1))

    level = one(*pieces[0])
    for cut in pieces[1:]:
        level = level * one(*cut)
    return level


def bell_draw(stream_key, dims, scale, limit, shards=(), kind=jnp.bfloat16):
    result = jax.random.normal(stream_key, dims, jnp.float32) * scale
    if len(shards) > 0:
        result = steps_of(stream_key, dims, shards, -0.22, 0.18) * result
    return jnp.clip(result, min=-limit, max=limit).astype(kind)


def setup_inputs(seed: int = 0) -> dict:
    keys = jax.random.split(jax.random.key(seed), 6)
    panels = draw_panels(jax.random.fold_in(keys[5], 71), 0)
    shapes = bell_draw(keys[1], (NDOF, M), M ** -0.5, 0.09375, ((0, 16),))
    harmonic = draw_harmonic(jax.random.fold_in(keys[5], 71), 0)
    connect = draw_connect(jax.random.fold_in(keys[5], 71), 0)
    recovery = bell_draw(keys[4], (ELEMS, CORNERS), 0.5, 3.0, ((0, 32),), jnp.float32)
    return {"panels": panels, "shapes": shapes, "harmonic": harmonic, "connect": connect, "recovery": recovery}


def spectral_tables(harmonic):
    step_ids = jnp.arange(STEPS, dtype=jnp.int32)
    phases = harmonic[:, None] * step_ids[None, :] % HARM
    angles = phases.astype(jnp.float32) * (2.0 * math.pi / HARM)
    ratios = harmonic.astype(jnp.float32) / HARM
    squared = ratios * ratios
    weights = jnp.stack([jnp.ones_like(ratios), ratios, squared, squared * squared]) / F
    return (jnp.cos(angles), jnp.sin(angles), weights)

def reference(panels, shapes, harmonic, connect, recovery):
    cos_table, sin_table, weights = spectral_tables(harmonic)
    norm_scale = math.sqrt(2.0 / F)
    highest = lax.Precision.HIGHEST
    panel_real = panels[0].astype(jnp.float32)
    panel_imag = panels[1].astype(jnp.float32)

    def group_rows(group_index):
        shape_rows = lax.dynamic_slice_in_dim(shapes, group_index * ROWS_MODE, ROWS_MODE, 0).astype(jnp.float32)
        real_part = jnp.dot(panel_real, shape_rows.T, precision=highest)
        imag_part = jnp.dot(panel_imag, shape_rows.T, precision=highest)
        history = norm_scale * (jnp.dot(real_part.T, cos_table, precision=highest) - jnp.dot(imag_part.T, sin_table, precision=highest))
        power_rows = real_part * real_part + imag_part * imag_part
        return (history.astype(jnp.bfloat16), jnp.dot(weights, power_rows, precision=highest))
    histories, moments = lax.map(group_rows, jnp.arange(N_MODE, dtype=jnp.int32))
    history_wide = histories.reshape(NDOF, STEPS).astype(jnp.float32)
    moments = jnp.transpose(moments, (1, 0, 2)).reshape(4, NDOF)
    stress = jnp.zeros((ELEMS, STEPS), jnp.float32)
    for corner in range(CORNERS):
        stress = stress + recovery[:, corner:corner + 1] * jnp.take(history_wide, connect[:, corner], axis=0)
    return (stress, moments)
```

```python
import functools
import math

import jax
import jax.numpy as jnp
from jax import lax
from jax.experimental import pallas as pl
from jax.experimental.pallas import tpu as pltpu
from jax.sharding import PartitionSpec as P

HARM = 4096
F32 = jnp.float32
BF16 = jnp.bfloat16


def split(value):
    head = lax.reduce_precision(value, 8, 7)
    return head.astype(BF16), (value - head).astype(BF16)


def moment_weights(harmonic, lines):
    ratios = harmonic.astype(F32) / HARM
    squared = ratios * ratios
    return jnp.stack([jnp.ones_like(ratios), ratios, squared, squared * squared]) / lines


def nt(a, b):
    return lax.dot_general(a, b, (((1,), (1,)), ((), ())), preferred_element_type=F32)


def nn(a, b):
    return jnp.dot(a, b, preferred_element_type=F32)


def kernel_split(value):
    head = value.astype(BF16)
    return head, (value - head.astype(F32)).astype(BF16)


def step_body(count, spectra_on, time_on, carried, idx_ref, *refs):
    refs = list(refs)
    take = lambda n: [refs.pop(0) for _ in range(n)]
    panels = take(count)
    if spectra_on:
        own, other = take(count), take(count)
    if time_on:
        v_head, v_tail = take(count), take(count)
        t_head, t_tail = take(2)
    spectra_in = take(1)[0] if spectra_on and carried else None
    stress_in = take(1)[0] if time_on and carried else None
    spectra_out = take(1)[0] if spectra_on else None
    stress_out = take(1)[0] if time_on else None
    grids = take(count) if time_on else None

    step = pl.program_id(0) * pl.num_programs(1) + pl.program_id(1)
    last = pl.num_programs(0) * pl.num_programs(1) - 1
    if spectra_on:
        rows = own[0].shape[0]
        for part, table in ((0, own), (1, other)):
            here = pl.ds(part * rows, rows)
            total = spectra_in[0, here, :] if carried else None
            for shape_ref, panel in zip(table, panels):
                term = nt(shape_ref[...], panel[0])
                total = term if total is None else total + term
            spectra_out[0, here, :] = total
    if time_on:
        for panel, grid in zip(panels, grids):
            term = nn(t_head[...], panel[0]) + nn(t_tail[...], panel[0])

            @pl.when(step == 0)
            def _():
                grid[...] = term

            @pl.when(step > 0)
            def _():
                grid[...] += term

        @pl.when(step == last)
        def _():
            total = stress_in[...] if carried else None
            for head, tail, grid in zip(v_head, v_tail, grids):
                g_head, g_tail = kernel_split(grid[...])
                term = nt(head[...], g_head) + nt(tail[...], g_head) + nt(head[...], g_tail)
                total = term if total is None else total + term
            stress_out[...] = total


def block_step(blocks, cols, shapes, v, t, spectra, stress, spectra_on=True, time_on=True):
    count = len(blocks)
    parts, lines, modes = blocks[0].shape
    rows = shapes[0].shape[0]
    elems, steps = v[0].shape[0], t[0].shape[0]
    carried = (spectra if spectra_on else stress) is not None
    tile = min(lines, 256)
    tiles = lines // tile

    def col(b):
        return lambda i, j, idx: (0, idx[b])

    in_specs = [pl.BlockSpec((1, tile, modes), lambda i, j, idx: (i, j, 0))] * count
    args = list(blocks)
    flops = bytes_moved = 0
    if spectra_on:
        for table in shapes:
            in_specs += [pl.BlockSpec((rows, modes), col(b)) for b in range(count)]
            args += [table] * count
        flops += 2 * count * parts * lines * modes * 2 * rows
        bytes_moved += 2 * parts * 2 * rows * lines * 4
    if time_on:
        for table in v:
            in_specs += [pl.BlockSpec((elems, modes), col(b)) for b in range(count)]
            args += [table] * count
        in_specs += [pl.BlockSpec((steps, tile), lambda i, j, idx: (0, i * tiles + j))] * 2
        args += list(t)
        flops += count * 2 * modes * steps * (2 * parts * lines + 3 * elems)
        bytes_moved += 2 * elems * steps * 4
    spectra_spec = pl.BlockSpec((1, 2 * rows, tile), lambda i, j, idx: (i, 0, j))
    stress_spec = pl.BlockSpec((elems, steps), lambda i, j, idx: (0, 0))
    out_specs, out_shape, aliases = [], [], {}
    if spectra_on:
        if carried:
            aliases[len(args) + 1] = len(out_specs)
            in_specs.append(spectra_spec)
            args.append(spectra)
        out_specs.append(spectra_spec)
        out_shape.append(jax.ShapeDtypeStruct((parts, 2 * rows, lines), F32))
    if time_on:
        if carried:
            aliases[len(args) + 1] = len(out_specs)
            in_specs.append(stress_spec)
            args.append(stress)
        out_specs.append(stress_spec)
        out_shape.append(jax.ShapeDtypeStruct((elems, steps), F32))
    return pl.pallas_call(
        functools.partial(step_body, count, spectra_on, time_on, carried),
        out_shape=out_shape,
        grid_spec=pltpu.PrefetchScalarGridSpec(
            num_scalar_prefetch=1,
            grid=(parts, tiles),
            in_specs=in_specs,
            out_specs=out_specs,
            scratch_shapes=[pltpu.VMEM((steps, modes), F32)] * (count if time_on else 0),
        ),
        input_output_aliases=aliases,
        compiler_params=pltpu.CompilerParams(vmem_limit_bytes=40 << 20),
        cost_estimate=pl.CostEstimate(
            flops=flops, bytes_accessed=bytes_moved + count * parts * lines * modes * 2, transcendentals=0
        ),
        name="block_step",
    )(cols, *args)


def moment_body(count, idx_ref, *refs):
    refs = list(refs)
    take = lambda n: [refs.pop(0) for _ in range(n)]
    panels, own, other = take(count), take(count), take(count)
    w_head, w_tail, spectra, out = refs
    rows = own[0].shape[0]
    for part, table in ((0, own), (1, other)):
        here = pl.ds(part * rows, rows)
        power = None
        for c in range(2):
            total = spectra[c, here, :]
            for shape_ref, panel in zip(table, panels):
                total = total + nt(shape_ref[...], panel[c])
            power = total * total if power is None else power + total * total
        p_head, p_tail = kernel_split(power)
        term = nt(w_head[...], p_head) + nt(w_tail[...], p_head) + nt(w_head[...], p_tail)

        @pl.when(pl.program_id(0) == 0)
        def _():
            out[:, here] = term

        @pl.when(pl.program_id(0) > 0)
        def _():
            out[:, here] += term


def block_moments(blocks, cols, shapes, weights, spectra):
    count = len(blocks)
    parts, lines, modes = blocks[0].shape
    rows = shapes[0].shape[0]
    tile = min(lines, 128)

    def col(b):
        return lambda j, idx: (0, idx[b])

    in_specs = [pl.BlockSpec((parts, tile, modes), lambda j, idx: (0, j, 0))] * count
    args = list(blocks)
    for table in shapes:
        in_specs += [pl.BlockSpec((rows, modes), col(b)) for b in range(count)]
        args += [table] * count
    in_specs += [pl.BlockSpec((weights[0].shape[0], tile), lambda j, idx: (0, j))] * 2
    in_specs.append(pl.BlockSpec((parts, 2 * rows, tile), lambda j, idx: (0, 0, j)))
    args += [*weights, spectra]
    return pl.pallas_call(
        functools.partial(moment_body, count),
        out_shape=jax.ShapeDtypeStruct((weights[0].shape[0], 2 * rows), F32),
        grid_spec=pltpu.PrefetchScalarGridSpec(
            num_scalar_prefetch=1,
            grid=(lines // tile,),
            in_specs=in_specs,
            out_specs=pl.BlockSpec((weights[0].shape[0], 2 * rows), lambda j, idx: (0, 0)),
        ),
        compiler_params=pltpu.CompilerParams(vmem_limit_bytes=40 << 20),
        cost_estimate=pl.CostEstimate(
            flops=2 * count * parts * lines * modes * 2 * rows,
            bytes_accessed=parts * 2 * rows * lines * 4,
            transcendentals=0,
        ),
        name="block_moments",
    )(cols, *args)


def paired_shards(n_mode, panels, shapes, harmonic, connect, recovery, *, steps):
    tie = lax.optimization_barrier
    place = lax.axis_index("mode")
    core, side, layer = place % 2, place // 2 % 2, place // 4
    layers = n_mode // 4
    ring = lambda a: lax.ppermute(a, "mode", [(i, (i + 4) % n_mode) for i in range(n_mode)])
    across = lambda a: lax.ppermute(a, "mode", [(i, i ^ 2) for i in range(n_mode)])
    mate = lambda a: lax.ppermute(a, "mode", [(i, i ^ 1) for i in range(n_mode)])
    peer = lambda a: lax.ppermute(a, "node", [(0, 1), (1, 0)])

    lines = panels.shape[1] // 2
    total_lines = panels.shape[1] * 2
    rows = shapes.shape[0]
    parts, _, modes = panels.shape
    mine = lax.dynamic_slice(panels, (0, core * lines, 0), (parts, lines, modes))
    theirs = lax.dynamic_slice(panels, (0, (1 - core) * lines, 0), (parts, lines, modes))

    z = [[mine], [mate(theirs)]]
    x = [[], []]
    for s in range(layers - 1):
        for h in range(2):
            moved, swapped = tie((ring(z[h][-1]), across(z[h][-1])))
            z[h].append(moved)
            x[h].append(swapped)
    final = [across(z[0][-1]), ring(x[1][-1])]

    def cols(*wanted):
        out = []
        for back, flip, h in wanted:
            at = (layer - back) % layers
            xs = 1 - side if flip else side
            cs = 1 - core if h else core
            out.append((at * 2 + xs) * 2 + cs)
        return jnp.stack(out).astype(jnp.int32)

    local = (connect - place * rows).astype(F32)
    packed = jnp.stack([local.T, recovery.T])
    own_pair = jnp.concatenate([packed, peer(packed)], axis=2)
    other_pair = mate(own_pair)
    other_shapes = mate(shapes)
    slots = jnp.arange(rows, dtype=jnp.int32).astype(F32)
    v_parts = []
    for pair, table in ((own_pair, shapes), (other_pair, other_shapes)):
        hit = pair[0][:, None, :] == slots[None, :, None]
        weight = jnp.sum(jnp.where(hit, pair[1][:, None, :], 0.0), axis=0)
        dims = (((0,), (0,)), ((), ()))
        v_parts.append(
            sum(lax.dot_general(w, table, dims, preferred_element_type=F32) for w in split(weight))
        )
    v = split(jnp.concatenate(v_parts, axis=0))

    mine_h = lax.dynamic_slice(harmonic, (core * lines,), (lines,))
    step_ids = jnp.arange(steps, dtype=jnp.int32)
    phases = step_ids[:, None] * mine_h[None, :] % HARM
    angles = phases.astype(F32) * (2.0 * math.pi / HARM)
    scale = math.sqrt(2.0 / total_lines)
    table = jnp.concatenate([scale * jnp.cos(angles), -scale * jnp.sin(angles)], axis=1)
    t = split(table)
    weights = split(jnp.pad(moment_weights(mine_h, total_lines), ((0, 4), (0, 0))))

    both = (shapes, other_shapes)
    spectra, stress = block_step(
        [z[0][0], z[1][0]], cols((0, 0, 0), (0, 0, 1)), both, v, t, None, None
    )
    for s in range(layers - 1):
        for h in range(2):
            spectra, stress = block_step(
                [x[h][s], z[h][s + 1]], cols((s, 1, h), (s + 1, 0, h)), both, v, t, spectra, stress
            )
    ends = cols((layers - 1, 1, 0), (layers - 1, 1, 1))
    (stress,) = block_step(final, ends, both, v, t, None, stress, spectra_on=False)
    moments = block_moments(final, ends, both, weights, spectra)

    elems = connect.shape[0]
    keep, give = stress[: 2 * elems], stress[2 * elems :]
    keep = keep + mate(give)
    stress = keep[:elems] + peer(keep[elems:])
    half = moments[:, :rows] + mate(moments[:, rows:])
    node = lax.axis_index("node")
    mine_m = lax.dynamic_slice(half, (0, node * (rows // 2)), (8, rows // 2))
    give_m = lax.dynamic_slice(half, (0, (1 - node) * (rows // 2)), (8, rows // 2))
    moments = mine_m + peer(give_m)
    return stress, moments[:4]


def plain_shards(panels, shapes, harmonic, connect, recovery, *, steps, total_lines):
    highest = lax.Precision.HIGHEST
    rows_mode = shapes.shape[0]
    spectra = jnp.einsum(
        "cfm,rm->cfr",
        lax.all_gather(panels, "mode", axis=2, tiled=True),
        shapes,
        preferred_element_type=F32,
    )
    step_ids = jnp.arange(steps, dtype=jnp.int32)
    phases = harmonic[:, None] * step_ids[None, :] % HARM
    angles = phases.astype(F32) * (2.0 * math.pi / HARM)
    weights = moment_weights(harmonic, total_lines)
    history = jnp.einsum("fr,ft->rt", spectra[0], jnp.cos(angles), precision=highest)
    history = history - jnp.einsum("fr,ft->rt", spectra[1], jnp.sin(angles), precision=highest)
    power = spectra[0] * spectra[0] + spectra[1] * spectra[1]
    history = math.sqrt(2.0 / total_lines) * history
    moments = jnp.dot(weights, power, precision=highest)
    history = lax.psum_scatter(history, "node", scatter_dimension=0, tiled=True)
    moments = lax.psum_scatter(moments, "node", scatter_dimension=1, tiled=True)
    rows_in = lax.all_gather(history.astype(BF16), "node", axis=0, tiled=True)
    local = connect - lax.axis_index("mode") * rows_mode
    slots = jnp.arange(rows_mode, dtype=jnp.int32)
    hit = local[:, :, None] == slots[None, None, :]
    weight = jnp.sum(jnp.where(hit, recovery[:, :, None], 0.0), axis=1)
    stress = jnp.dot(weight, rows_in, preferred_element_type=F32, precision=highest)
    return stress, moments


STEPS = 512


def solution(mesh):
    n_mode, n_node = mesh.shape["mode"], mesh.shape["node"]

    def shards(panels, *rest):
        if n_node == 2 and n_mode % 4 == 0 and n_mode >= 8:
            return paired_shards(n_mode, panels, *rest, steps=STEPS)
        return plain_shards(panels, *rest, steps=STEPS, total_lines=panels.shape[1] * n_node)

    return jax.shard_map(
        shards,
        mesh=mesh,
        in_specs=(
            P(None, "node", "mode"),
            P("mode", None),
            P("node"),
            P(("mode", "node"), None),
            P(("mode", "node"), None),
        ),
        out_specs=(P(("mode", "node"), None), P(None, ("mode", "node"))),
        check_vma=False,
    )
```

```python
import functools
import math

import jax
import jax.numpy as jnp
from jax import lax
from jax.experimental import pallas as pl
from jax.experimental.pallas import tpu as pltpu
from jax.sharding import PartitionSpec as P

HARM = 4096
F32 = jnp.float32
BF16 = jnp.bfloat16


def split(value):
    head = lax.reduce_precision(value, 8, 7)
    return head.astype(BF16), (value - head).astype(BF16)


def moment_weights(harmonic, lines):
    ratios = harmonic.astype(F32) / HARM
    squared = ratios * ratios
    return jnp.stack([jnp.ones_like(ratios), ratios, squared, squared * squared]) / lines


def nt(a, b):
    return lax.dot_general(a, b, (((1,), (1,)), ((), ())), preferred_element_type=F32)


def nn(a, b):
    return jnp.dot(a, b, preferred_element_type=F32)


def kernel_split(value):
    head = value.astype(BF16)
    return head, (value - head.astype(F32)).astype(BF16)


VMEM = pl.BlockSpec(memory_space=pltpu.VMEM)
SMEM = pl.BlockSpec(memory_space=pltpu.SMEM)


def on_chip(body, out_shapes, operands, name, aliases=None):
    outs = [pltpu.VMEM(shape, dtype) for shape, dtype in out_shapes]
    return pl.pallas_call(
        body,
        out_shape=outs,
        in_specs=[SMEM] + [VMEM] * (len(operands) - 1),
        out_specs=[VMEM] * len(outs),
        input_output_aliases=aliases or {},
        compiler_params=pltpu.CompilerParams(vmem_limit_bytes=16 << 20),
        cost_estimate=pl.CostEstimate(flops=1000, bytes_accessed=1000, transcendentals=0),
        name=name,
    )(*operands)


def column(ref, index, modes, here=slice(None)):
    return ref[here, pl.ds(pl.multiple_of(index * modes, modes), modes)]


def added(total, blocks, first, idx, shape_refs, here):
    for b, panel in enumerate(blocks):
        parts, lines, modes = panel.shape
        flat = panel[...].reshape(parts * lines, modes)
        term = nt(flat, column(shape_refs, idx[first + b], modes, here))
        total = term if total is None else total + term
    return total


def row_tiles(shape_refs):
    for g, table in enumerate(shape_refs):
        rows = table.shape[0]
        width = min(rows, 256)
        for r in range(0, rows, width):
            yield table, pl.ds(r, width), pl.ds(g * rows + r, width)


def spectra_body(first, count, carried, idx, own, other, *refs):
    blocks, out = refs[:count], refs[-1]
    parts, lines, _ = out.shape
    for table, here, there in row_tiles((own, other)):
        total = out[:, :, there].reshape(parts * lines, -1) if carried else None
        total = added(total, blocks, first, idx, table, here)
        out[:, :, there] = total.reshape(parts, lines, -1)


def add_spectra(blocks, first, idx, both, spectra):
    parts, lines, _ = blocks[0].shape
    operands = [idx, *both, *blocks]
    aliases = {}
    if spectra is not None:
        aliases = {len(operands): 0}
        operands.append(spectra)
    body = functools.partial(spectra_body, first, len(blocks), spectra is not None)
    shape = (parts, lines, 2 * both[0].shape[0])
    return on_chip(body, [(shape, F32)], operands, "add_spectra", aliases)[0]


def table_body(idx, harmonic, t_head, t_tail, weights):
    steps, both = t_head.shape
    lines = both // 2
    total_lines = harmonic.shape[1] * 2
    mine = harmonic[:, pl.ds(pl.multiple_of(idx[0] * lines, lines), lines)]
    ratios = mine.astype(F32) * (1.0 / HARM)
    squared = ratios * ratios
    ones = jnp.ones_like(ratios)
    rows = [ones, ratios, squared, squared * squared] * 2
    weights[...] = (jnp.concatenate(rows, axis=0) * (1.0 / total_lines)).T
    scale = math.sqrt(2.0 / total_lines)
    tile = 64
    for j in range(0, steps, tile):
        ids = lax.broadcasted_iota(jnp.int32, (tile, lines), 0) + j
        angles = ((ids * mine) & (HARM - 1)).astype(F32) * (2.0 * math.pi / HARM)
        here = slice(j, j + tile)
        for at, value in ((0, scale * jnp.cos(angles)), (lines, -scale * jnp.sin(angles))):
            head, tail = kernel_split(value)
            t_head[here, at : at + lines] = head
            t_tail[here, at : at + lines] = tail


def weights_body(first, idx, own, other, *refs):
    pairs, (w_head, w_tail, v_head, v_tail) = refs[:4], refs[4:]
    elems = pairs[0].shape[2]
    modes = v_head.shape[1] // 2
    rows = own.shape[0]
    slots = lax.broadcasted_iota(jnp.int32, (elems, rows), 1).astype(F32)
    for p, pair in enumerate(pairs):
        local, value = pair[0].T, pair[1].T
        weight = jnp.zeros((elems, rows), F32)
        for k in range(local.shape[1]):
            weight += jnp.where(local[:, k : k + 1] == slots, value[:, k : k + 1], 0.0)
        head, tail = kernel_split(weight)
        here = slice(p * elems, (p + 1) * elems)
        w_head[here, :] = head
        w_tail[here, :] = tail
    for g, table in enumerate((own, other)):
        here = slice(2 * g * elems, 2 * (g + 1) * elems)
        for b in range(2):
            part = column(table, idx[first + b], modes)
            head, tail = kernel_split(nn(w_head[here, :], part) + nn(w_tail[here, :], part))
            v_head[here, b * modes : (b + 1) * modes] = head
            v_tail[here, b * modes : (b + 1) * modes] = tail


def stress_body(idx, spectra, w_head, w_tail, t_head, t_tail, out):
    parts, lines, both = spectra.shape
    rows, elems = both // 2, out.shape[0] // 2
    for g in range(2):
        here = slice(g * elems, (g + 1) * elems)
        values = spectra[:, :, g * rows : (g + 1) * rows].reshape(parts * lines, rows)
        s_head, s_tail = kernel_split(values)
        w_h = w_head[here, :]
        picked = nt(w_h, s_head) + nt(w_h, s_tail) + nt(w_tail[here, :], s_head)
        p_head, p_tail = kernel_split(picked)
        t_h = t_head[...]
        out[here, :] = nt(p_head, t_h) + nt(p_tail, t_h) + nt(p_head, t_tail[...])


def last_body(idx, panel_a, panel_b, v_head, v_tail, t_head, t_tail, before, keep, give):
    total = before[...]
    for b, panel in enumerate((panel_a, panel_b)):
        parts, lines, modes = panel.shape
        here = slice(b * modes, (b + 1) * modes)
        flat = panel[...].reshape(parts * lines, modes)
        g_head, g_tail = kernel_split(nn(t_head[...], flat) + nn(t_tail[...], flat))
        head = v_head[:, here]
        total += nt(head, g_head) + nt(v_tail[:, here], g_head) + nt(head, g_tail)
    half = total.shape[0] // 2
    keep[...] = total[:half]
    give[...] = total[half:]


def moment_body(first, idx, own, other, panel_a, panel_b, spectra, weights, keep, give):
    parts, lines, _ = spectra.shape
    rows = own.shape[0]
    for table, here, there in row_tiles((own, other)):
        total = spectra[:, :, there].reshape(parts * lines, -1)
        total = added(total, (panel_a, panel_b), first, idx, table, here)
        total = total * total
        power = total[:lines] + total[lines:]
        sums = [jnp.sum(power * weights[:, k : k + 1], axis=0, keepdims=True) for k in range(4)]
        out = keep if there.start < rows else give
        out[:, here] = jnp.concatenate(sums + sums, axis=0)


def paired_shards(n_mode, panels, shapes, harmonic, connect, recovery, *, steps):
    tie = lax.optimization_barrier
    place = lax.axis_index("mode")
    core, side, layer = place % 2, place // 2 % 2, place // 4
    layers = n_mode // 4
    ring = lambda a: lax.ppermute(a, "mode", [(i, (i + 4) % n_mode) for i in range(n_mode)])
    across = lambda a: lax.ppermute(a, "mode", [(i, i ^ 2) for i in range(n_mode)])
    mate = lambda a: lax.ppermute(a, "mode", [(i, i ^ 1) for i in range(n_mode)])
    peer = lambda a: lax.ppermute(a, "node", [(0, 1), (1, 0)])

    parts, both_lines, modes = panels.shape
    lines = both_lines // 2
    rows = shapes.shape[0]
    elems = connect.shape[0]

    wanted = [(0, 0, 0), (0, 0, 1)]
    for s in range(layers - 1):
        for h in range(2):
            wanted += [(s, 1, h), (s + 1, 0, h)]
    wanted += [(layers - 1, 1, 0), (layers - 1, 1, 1)]
    back, flip, half = (jnp.array(column, dtype=jnp.int32) for column in zip(*wanted))
    index = (((layer - back) % layers) * 2 + (side + flip) % 2) * 2 + (core + half) % 2
    idx = jnp.concatenate([core[None], index]).astype(jnp.int32)
    last = len(wanted) - 1

    mine = lax.dynamic_slice(panels, (0, core * lines, 0), (parts, lines, modes))
    theirs = lax.dynamic_slice(panels, (0, (1 - core) * lines, 0), (parts, lines, modes))
    z = [[mine], [mate(theirs)]]
    x = [[], []]
    z[1][0], shapes_in = tie((z[1][0], shapes))
    both = (shapes, mate(shapes_in))

    def prepare(idx, harmonic, connect, recovery):
        table = [((steps, 2 * lines), BF16)] * 2 + [((lines, 8), F32)]
        *t, weights = on_chip(table_body, table, [idx, harmonic.reshape(1, -1)], "table")
        packed = jnp.stack([(connect - place * rows).astype(F32).T, recovery.T])
        across_node = peer(packed)
        pairs = [packed, across_node, mate(packed), mate(across_node)]
        return t, weights, pairs

    spectra = None
    at = 1
    for s in range(layers - 1):
        for h in range(2):
            moved, swapped = ring(z[h][-1]), across(z[h][-1])
            if s == 0 and h == 0:
                moved, swapped, idx, harmonic, connect, recovery = tie(
                    (moved, swapped, idx, harmonic, connect, recovery)
                )
                t, weights, pairs = prepare(idx, harmonic, connect, recovery)
                spectra = add_spectra([z[0][0], z[1][0]], at, idx, both, None)
                at += 2
            elif s == 1 and h == 0:
                moved, swapped, spectra, t, weights, pairs = tie(
                    (moved, swapped, spectra, t, weights, pairs)
                )
                shape = (4 * elems, rows), (4 * elems, 2 * modes)
                outs = [(shape[0], BF16)] * 2 + [(shape[1], BF16)] * 2
                body = functools.partial(weights_body, last)
                w_and_v = on_chip(body, outs, [idx, *both, *pairs], "weights")
            elif s == 2 and h == 0:
                moved, swapped, spectra, w_and_v = tie((moved, swapped, spectra, w_and_v))
            else:
                moved, swapped, spectra = tie((moved, swapped, spectra))
            z[h].append(moved)
            x[h].append(swapped)
            spectra = add_spectra([swapped, moved], at, idx, both, spectra)
            at += 2
    final = [across(z[0][-1]), ring(x[1][-1])]
    w, v = w_and_v[:2], w_and_v[2:]
    shape = (4 * elems, steps)
    (stress,) = on_chip(stress_body, [(shape, F32)], [idx, spectra, *w, *t], "first_stress")
    final[0], final[1], stress, spectra = tie((final[0], final[1], stress, spectra))
    part = [((2 * elems, steps), F32)] * 2
    keep, give = on_chip(last_body, part, [idx, *final, *v, *t, stress], "last_stress")
    give, spectra = tie((give, spectra))
    got = mate(give)
    part = [((8, rows), F32)] * 2
    body = functools.partial(moment_body, last)
    keep_m, give_m = on_chip(
        body, part, [idx, *both, *final, spectra, weights], "moments"
    )
    send = (keep[elems:] + got[elems:]).astype(BF16)
    half = keep_m + mate(give_m)
    stress = (keep[:elems] + got[:elems]) + peer(send).astype(F32)
    moments = half + peer(half)
    start = lax.axis_index("node") * (rows // 2)
    return stress, lax.dynamic_slice(moments, (0, start), (4, rows // 2))


def plain_shards(panels, shapes, harmonic, connect, recovery, *, steps, total_lines):
    highest = lax.Precision.HIGHEST
    rows_mode = shapes.shape[0]
    spectra = jnp.einsum(
        "cfm,rm->cfr",
        lax.all_gather(panels, "mode", axis=2, tiled=True),
        shapes,
        preferred_element_type=F32,
    )
    step_ids = jnp.arange(steps, dtype=jnp.int32)
    phases = harmonic[:, None] * step_ids[None, :] % HARM
    angles = phases.astype(F32) * (2.0 * math.pi / HARM)
    weights = moment_weights(harmonic, total_lines)
    history = jnp.einsum("fr,ft->rt", spectra[0], jnp.cos(angles), precision=highest)
    history = history - jnp.einsum("fr,ft->rt", spectra[1], jnp.sin(angles), precision=highest)
    power = spectra[0] * spectra[0] + spectra[1] * spectra[1]
    history = math.sqrt(2.0 / total_lines) * history
    moments = jnp.dot(weights, power, precision=highest)
    history = lax.psum_scatter(history, "node", scatter_dimension=0, tiled=True)
    moments = lax.psum_scatter(moments, "node", scatter_dimension=1, tiled=True)
    rows_in = lax.all_gather(history.astype(BF16), "node", axis=0, tiled=True)
    local = connect - lax.axis_index("mode") * rows_mode
    slots = jnp.arange(rows_mode, dtype=jnp.int32)
    hit = local[:, :, None] == slots[None, None, :]
    weight = jnp.sum(jnp.where(hit, recovery[:, :, None], 0.0), axis=1)
    stress = jnp.dot(weight, rows_in, preferred_element_type=F32, precision=highest)
    return stress, moments


STEPS = 512


def solution(mesh):
    n_mode, n_node = mesh.shape["mode"], mesh.shape["node"]

    def shards(panels, *rest):
        if n_node == 2 and n_mode % 4 == 0 and n_mode >= 8:
            return paired_shards(n_mode, panels, *rest, steps=STEPS)
        return plain_shards(panels, *rest, steps=STEPS, total_lines=panels.shape[1] * n_node)

    return jax.shard_map(
        shards,
        mesh=mesh,
        in_specs=(
            P(None, "node", "mode"),
            P("mode", None),
            P("node"),
            P(("mode", "node"), None),
            P(("mode", "node"), None),
        ),
        out_specs=(P(("mode", "node"), None), P(None, ("mode", "node"))),
        check_vma=False,
    )
```

```python
import functools
import math

import jax
import jax.numpy as jnp
from jax import lax
from jax.experimental import pallas as pl
from jax.experimental.pallas import tpu as pltpu
from jax.sharding import PartitionSpec as P

HARM = 4096
F32 = jnp.float32
BF16 = jnp.bfloat16


def split(value):
    head = lax.reduce_precision(value, 8, 7)
    return head.astype(BF16), (value - head).astype(BF16)


def moment_weights(harmonic, lines):
    ratios = harmonic.astype(F32) / HARM
    squared = ratios * ratios
    return jnp.stack([jnp.ones_like(ratios), ratios, squared, squared * squared]) / lines


def nt(a, b):
    return lax.dot_general(a, b, (((1,), (1,)), ((), ())), preferred_element_type=F32)


def nn(a, b):
    return jnp.dot(a, b, preferred_element_type=F32)


def kernel_split(value):
    head = value.astype(BF16)
    return head, (value - head.astype(F32)).astype(BF16)


VMEM = pl.BlockSpec(memory_space=pltpu.VMEM)
SMEM = pl.BlockSpec(memory_space=pltpu.SMEM)
HBM = pl.BlockSpec(memory_space=pltpu.HBM)


def on_chip(
    body, out_shapes, idx, operands, name, both=(), columns=0, modes=0, aliases=None, keep_columns=False
):
    outs = [pltpu.VMEM(shape, dtype) for shape, dtype in out_shapes]
    scratch = []
    if both:
        rows = both[0].shape[0]
        scratch = [pltpu.SemaphoreType.DMA((2, columns))]
        if not keep_columns:
            scratch.insert(0, pltpu.VMEM((2, columns, rows, modes), BF16))
    aliases = {1 + len(both) + i: o for i, o in (aliases or {}).items()}
    return pl.pallas_call(
        body,
        out_shape=outs,
        in_specs=[SMEM] + [HBM] * len(both) + [VMEM] * len(operands),
        out_specs=[VMEM] * len(outs),
        scratch_shapes=scratch,
        input_output_aliases=aliases,
        compiler_params=pltpu.CompilerParams(vmem_limit_bytes=16 << 20),
        cost_estimate=pl.CostEstimate(flops=1000, bytes_accessed=1000, transcendentals=0),
        name=name,
    )(idx, *both, *operands)


def pinned(value):
    return pltpu.with_memory_space_constraint(value, pltpu.VMEM)


def fetch(idx, first, both, buffer, sems):
    _, columns, _, modes = buffer.shape
    copies = {}
    for g, table in enumerate(both):
        for b in range(columns):
            at = pl.ds(pl.multiple_of(idx[first + b] * modes, modes), modes)
            copies[g, b] = pltpu.make_async_copy(table.at[:, at], buffer.at[g, b], sems.at[g, b])
    for copy in copies.values():
        copy.start()
    return copies


def row_tiles(rows):
    width = min(rows, 256)
    for g in range(2):
        for r in range(0, rows, width):
            yield g, pl.ds(r, width), pl.ds(g * rows + r, width)


def flat(panel):
    if isinstance(panel, tuple):
        return jnp.concatenate([part[0] for part in panel], axis=0)
    return panel[...].reshape(-1, panel.shape[2])


def spectra_body(first, count, carried, idx, own, other, *refs):
    blocks, (out, buffer, sems) = refs[:count], refs[-3:]
    parts, lines, _ = out.shape
    copies = fetch(idx, first, (own, other), buffer, sems)
    for g, here, there in row_tiles(own.shape[0]):
        if here.start == 0:
            for b in range(count):
                copies[g, b].wait()
        total = out[:, :, there].reshape(parts * lines, -1) if carried else None
        for b, panel in enumerate(blocks):
            term = nt(flat(panel), buffer[g, b, here, :])
            total = term if total is None else total + term
        out[:, :, there] = total.reshape(parts, lines, -1)


def add_spectra(blocks, first, idx, both, spectra):
    parts, lines, modes = blocks[0].shape
    count = len(blocks)
    operands, aliases = list(blocks), {}
    if spectra is not None:
        aliases = {count: 0}
        operands.append(pinned(spectra))
    body = functools.partial(spectra_body, first, count, spectra is not None)
    shape = (parts, lines, 2 * both[0].shape[0])
    return on_chip(
        body, [(shape, F32)], idx, operands, "add_spectra", both, count, modes, aliases
    )[0]


def table_body(idx, harmonic, t_head, t_tail, weights):
    steps, both = t_head.shape
    lines = both // 2
    total_lines = harmonic.shape[1] * 2
    mine = harmonic[:, pl.ds(pl.multiple_of(idx[0] * lines, lines), lines)]
    ratios = mine.astype(F32) * (1.0 / HARM)
    squared = ratios * ratios
    ones = jnp.ones_like(ratios)
    rows = [ones, ratios, squared, squared * squared] * 2
    weights[...] = (jnp.concatenate(rows, axis=0) * (1.0 / total_lines)).T
    scale = math.sqrt(2.0 / total_lines)
    tile = 64
    for j in range(0, steps, tile):
        ids = lax.broadcasted_iota(jnp.int32, (tile, lines), 0) + j
        angles = ((ids * mine) & (HARM - 1)).astype(F32) * (2.0 * math.pi / HARM)
        here = slice(j, j + tile)
        for at, value in ((0, scale * jnp.cos(angles)), (lines, -scale * jnp.sin(angles))):
            head, tail = kernel_split(value)
            t_head[here, at : at + lines] = head
            t_tail[here, at : at + lines] = tail


def weights_body(first, idx, own, other, *refs):
    pairs, (w_head, w_tail, v_head, v_tail, buffer, sems) = refs[:4], refs[4:]
    copies = fetch(idx, first, (own, other), buffer, sems)
    elems = pairs[0].shape[2]
    modes = v_head.shape[1] // 2
    rows = own.shape[0]
    slots = lax.broadcasted_iota(jnp.int32, (elems, rows), 1).astype(F32)
    for p, pair in enumerate(pairs):
        local, value = (pair[0] - idx[1 + p // 2].astype(F32)).T, pair[1].T
        weight = jnp.zeros((elems, rows), F32)
        for k in range(local.shape[1]):
            weight += jnp.where(local[:, k : k + 1] == slots, value[:, k : k + 1], 0.0)
        head, tail = kernel_split(weight)
        here = slice(p * elems, (p + 1) * elems)
        w_head[here, :] = head
        w_tail[here, :] = tail
    for g in range(2):
        here = slice(2 * g * elems, 2 * (g + 1) * elems)
        for b in range(2):
            copies[g, b].wait()
            part = buffer[g, b]
            head, tail = kernel_split(nn(w_head[here, :], part) + nn(w_tail[here, :], part))
            v_head[here, b * modes : (b + 1) * modes] = head
            v_tail[here, b * modes : (b + 1) * modes] = tail


def stress_body(idx, spectra, w_head, w_tail, t_head, t_tail, out):
    parts, lines, both = spectra.shape
    rows, elems = both // 2, out.shape[0] // 2
    for g in range(2):
        here = slice(g * elems, (g + 1) * elems)
        values = spectra[:, :, g * rows : (g + 1) * rows].reshape(parts * lines, rows)
        s_head, s_tail = kernel_split(values)
        w_h = w_head[here, :]
        picked = nt(w_h, s_head) + nt(w_h, s_tail) + nt(w_tail[here, :], s_head)
        p_head, p_tail = kernel_split(picked)
        t_h = t_head[...]
        out[here, :] = nt(p_head, t_h) + nt(p_tail, t_h) + nt(p_head, t_tail[...])


def time_term(panel, v_head, v_tail, t_head, t_tail):
    g_head, g_tail = kernel_split(nn(t_head[...], panel) + nn(t_tail[...], panel))
    return nt(v_head, g_head) + nt(v_tail, g_head) + nt(v_head, g_tail)


def half_body(idx, real, imag, v_head, v_tail, columns, t_head, t_tail, spectra, stress, spectra_out, stress_out):
    parts, lines, _ = spectra.shape
    panel = flat((real, imag))
    modes = panel.shape[1]
    for g, here, there in row_tiles(columns.shape[2]):
        total = spectra[:, :, there].reshape(parts * lines, -1) + nt(panel, columns[g, 0, here, :])
        spectra_out[:, :, there] = total.reshape(parts, lines, -1)
    term = time_term(panel, v_head[:, :modes], v_tail[:, :modes], t_head, t_tail)
    stress_out[...] = stress[...] + term


def last_body(idx, real, imag, v_head, v_tail, t_head, t_tail, before, keep, give):
    panel = flat((real, imag))
    modes = panel.shape[1]
    total = before[...] + time_term(panel, v_head[:, modes:], v_tail[:, modes:], t_head, t_tail)
    half = total.shape[0] // 2
    keep[...] = total[:half]
    give[...] = total[half:]


def moment_body(idx, real, imag, columns, spectra, weights, keep, give):
    parts, lines, _ = spectra.shape
    panel = flat((real, imag))
    for g, here, there in row_tiles(columns.shape[2]):
        total = spectra[:, :, there].reshape(parts * lines, -1) + nt(panel, columns[g, 1, here, :])
        total = total * total
        power = total[:lines] + total[lines:]
        sums = [jnp.sum(power * weights[:, k : k + 1], axis=0, keepdims=True) for k in range(4)]
        (give if g else keep)[:, here] = jnp.concatenate(sums + sums, axis=0)


def paired_shards(n_mode, panels, shapes, harmonic, connect, recovery, *, steps):
    tie = lax.optimization_barrier
    place = lax.axis_index("mode")
    core, side, layer = place % 2, place // 2 % 2, place // 4
    layers = n_mode // 4
    ring = lambda a: lax.ppermute(a, "mode", [(i, (i + 4) % n_mode) for i in range(n_mode)])
    across = lambda a: lax.ppermute(a, "mode", [(i, i ^ 2) for i in range(n_mode)])
    mate = lambda a: lax.ppermute(a, "mode", [(i, i ^ 1) for i in range(n_mode)])
    peer = lambda a: lax.ppermute(a, "node", [(0, 1), (1, 0)])

    parts, both_lines, modes = panels.shape
    lines = both_lines // 2
    rows = shapes.shape[0]
    elems = connect.shape[0]

    wanted = [(0, 0, 0), (0, 0, 1)]
    for s in range(layers - 1):
        for h in range(2):
            wanted += [(s, 1, h), (s + 1, 0, h)]
    wanted += [(layers - 1, 1, 0), (layers - 1, 1, 1)]
    back, flip, half = (jnp.array(column, dtype=jnp.int32) for column in zip(*wanted))
    index = (((layer - back) % layers) * 2 + (side + flip) % 2) * 2 + (core + half) % 2
    bases = jnp.stack([core, place * rows, (place + 1 - 2 * core) * rows])
    last = len(wanted) + 1

    mine = lax.dynamic_slice(panels, (0, core * lines, 0), (parts, lines, modes))
    theirs = lax.dynamic_slice(panels, (0, (1 - core) * lines, 0), (parts, lines, modes))
    z = [[mine], [mate(theirs)]]
    x = [[], []]
    z[1][0], shapes_in, index, bases, harmonic, connect, recovery = tie(
        (z[1][0], shapes, index, bases, harmonic, connect, recovery)
    )
    idx = jnp.concatenate([bases, index]).astype(jnp.int32)
    packed = jnp.stack([connect.astype(F32).T, recovery.T])
    both = (shapes, mate(shapes_in))
    out = [((steps, 2 * lines), BF16)] * 2 + [((lines, 8), F32)]
    *t, weights = on_chip(table_body, out, idx, [harmonic.reshape(1, -1)], "table")
    across_node = peer(packed)
    pairs = [packed, across_node, mate(packed)]
    z[1][0], t, weights, pairs = tie((z[1][0], t, weights, pairs))
    pairs.append(mate(pairs[1]))
    spectra = None
    at = 3
    for s in range(layers - 1):
        for h in range(2):
            moved, swapped = ring(z[h][-1]), across(z[h][-1])
            if s == 0 and h == 0:
                moved, swapped = tie((moved, swapped))
                spectra = add_spectra([z[0][0], z[1][0]], at, idx, both, None)
                at += 2
            elif s == 1 and h == 0:
                moved, swapped, spectra, pairs = tie((moved, swapped, spectra, pairs))
                out = [((4 * elems, rows), BF16)] * 2 + [((4 * elems, 2 * modes), BF16)] * 2
                out.append(((2, 2, rows, modes), BF16))
                body = functools.partial(weights_body, last)
                w_and_v = on_chip(
                    body, out, idx, pairs, "weights", both, 2, modes, keep_columns=True
                )
            elif s == 2 and h == 0:
                moved, swapped, spectra, w_and_v = tie((moved, swapped, spectra, w_and_v))
            else:
                moved, swapped, spectra = tie((moved, swapped, spectra))
            z[h].append(moved)
            x[h].append(swapped)
            spectra = add_spectra([swapped, moved], at, idx, both, spectra)
            at += 2
    ends = [(across(z[h][-1][:1]), ring(x[h][-1][1:])) for h in range(2)]
    w, v, columns = [pinned(a) for a in w_and_v[:2]], [pinned(a) for a in w_and_v[2:4]], pinned(w_and_v[4])
    t = [pinned(a) for a in t]
    out = [((4 * elems, steps), F32)]
    (stress,) = on_chip(stress_body, out, idx, [pinned(spectra), *w, *t], "first_stress")
    ends[0], stress, spectra = tie((ends[0], stress, spectra))
    out.insert(0, (spectra.shape, F32))
    operands = [*ends[0], *v, columns, *t, pinned(spectra), pinned(stress)]
    spectra, stress = on_chip(half_body, out, idx, operands, "half_stress", aliases={7: 0, 8: 1})
    ends[1], stress, spectra = tie((ends[1], stress, spectra))
    out = [((2 * elems, steps), F32)] * 2
    keep, give = on_chip(last_body, out, idx, [*ends[1], *v, *t, pinned(stress)], "last_stress")
    give, spectra = tie((give, spectra))
    got = mate(give)
    out = [((8, rows), F32)] * 2
    operands = [*ends[1], columns, pinned(spectra), pinned(weights)]
    keep_m, give_m = on_chip(moment_body, out, idx, operands, "moments")
    send = (keep[elems:] + got[elems:]).astype(BF16)
    half = keep_m + mate(give_m)
    stress = (keep[:elems] + got[:elems]) + peer(send).astype(F32)
    moments = half + peer(half)
    start = lax.axis_index("node") * (rows // 2)
    return stress, lax.dynamic_slice(moments, (0, start), (4, rows // 2))


def plain_shards(panels, shapes, harmonic, connect, recovery, *, steps, total_lines):
    highest = lax.Precision.HIGHEST
    rows_mode = shapes.shape[0]
    spectra = jnp.einsum(
        "cfm,rm->cfr",
        lax.all_gather(panels, "mode", axis=2, tiled=True),
        shapes,
        preferred_element_type=F32,
    )
    step_ids = jnp.arange(steps, dtype=jnp.int32)
    phases = harmonic[:, None] * step_ids[None, :] % HARM
    angles = phases.astype(F32) * (2.0 * math.pi / HARM)
    weights = moment_weights(harmonic, total_lines)
    history = jnp.einsum("fr,ft->rt", spectra[0], jnp.cos(angles), precision=highest)
    history = history - jnp.einsum("fr,ft->rt", spectra[1], jnp.sin(angles), precision=highest)
    power = spectra[0] * spectra[0] + spectra[1] * spectra[1]
    history = math.sqrt(2.0 / total_lines) * history
    moments = jnp.dot(weights, power, precision=highest)
    history = lax.psum_scatter(history, "node", scatter_dimension=0, tiled=True)
    moments = lax.psum_scatter(moments, "node", scatter_dimension=1, tiled=True)
    rows_in = lax.all_gather(history.astype(BF16), "node", axis=0, tiled=True)
    local = connect - lax.axis_index("mode") * rows_mode
    slots = jnp.arange(rows_mode, dtype=jnp.int32)
    hit = local[:, :, None] == slots[None, None, :]
    weight = jnp.sum(jnp.where(hit, recovery[:, :, None], 0.0), axis=1)
    stress = jnp.dot(weight, rows_in, preferred_element_type=F32, precision=highest)
    return stress, moments


STEPS = 512


def solution(mesh):
    n_mode, n_node = mesh.shape["mode"], mesh.shape["node"]

    def shards(panels, *rest):
        if n_node == 2 and n_mode % 4 == 0 and n_mode >= 8:
            return paired_shards(n_mode, panels, *rest, steps=STEPS)
        return plain_shards(panels, *rest, steps=STEPS, total_lines=panels.shape[1] * n_node)

    return jax.shard_map(
        shards,
        mesh=mesh,
        in_specs=(
            P(None, "node", "mode"),
            P("mode", None),
            P("node"),
            P(("mode", "node"), None),
            P(("mode", "node"), None),
        ),
        out_specs=(P(("mode", "node"), None), P(None, ("mode", "node"))),
        check_vma=False,
    )
```

```python
import functools
import math

import jax
import jax.numpy as jnp
from jax import lax
from jax.experimental import pallas as pl
from jax.experimental.pallas import tpu as pltpu
from jax.sharding import PartitionSpec as P

HARM = 4096
F32 = jnp.float32
BF16 = jnp.bfloat16


def moment_weights(harmonic, lines):
    ratios = harmonic.astype(F32) / HARM
    squared = ratios * ratios
    return jnp.stack([jnp.ones_like(ratios), ratios, squared, squared * squared]) / lines


def nt(a, b):
    return lax.dot_general(a, b, (((1,), (1,)), ((), ())), preferred_element_type=F32)


def nn(a, b):
    return jnp.dot(a, b, preferred_element_type=F32)


def kernel_split(value):
    head = value.astype(BF16)
    return head, (value - head.astype(F32)).astype(BF16)


VMEM = pl.BlockSpec(memory_space=pltpu.VMEM)
HBM = pl.BlockSpec(memory_space=pltpu.HBM)


def on_chip(
    body, out_shapes, operands, name, both=(), columns=0, modes=0, aliases=None, keep_columns=False, flops=1000
):
    outs = [pltpu.VMEM(shape, dtype) for shape, dtype in out_shapes]
    scratch = []
    if both:
        rows = both[0].shape[0]
        scratch = [pltpu.SemaphoreType.DMA((2, columns))]
        if not keep_columns:
            scratch.insert(0, pltpu.VMEM((2, columns, rows, modes), BF16))
    aliases = {len(both) + i: o for i, o in (aliases or {}).items()}
    return pl.pallas_call(
        body,
        out_shape=outs,
        in_specs=[HBM] * len(both) + [VMEM] * len(operands),
        out_specs=[VMEM] * len(outs),
        scratch_shapes=scratch,
        input_output_aliases=aliases,
        compiler_params=pltpu.CompilerParams(vmem_limit_bytes=16 << 20),
        cost_estimate=pl.CostEstimate(flops=flops, bytes_accessed=1000, transcendentals=0),
        name=name,
    )(*both, *operands)


def pinned(value):
    return pltpu.with_memory_space_constraint(value, pltpu.VMEM)


def fetch(n_mode, wanted, both, buffer, sems):
    modes = buffer.shape[3]
    place = lax.axis_index("mode")
    layers = n_mode // 4
    layer, side, core = lax.div(place, 4), lax.rem(lax.div(place, 2), 2), lax.rem(place, 2)
    copies = {}
    for b, (back, flip, half) in enumerate(wanted):
        at = lax.rem(layer + (layers - back), layers) * 4
        at = at + lax.rem(side + flip, 2) * 2 + lax.rem(core + half, 2)
        at = pl.ds(pl.multiple_of(at * modes, modes), modes)
        for g, table in enumerate(both):
            copies[g, b] = pltpu.make_async_copy(table.at[:, at], buffer.at[g, b], sems.at[g, b])
    for copy in copies.values():
        copy.start()
    return copies


def row_tiles(rows):
    width = min(rows, 256)
    for g in range(2):
        for r in range(0, rows, width):
            yield g, pl.ds(r, width), pl.ds(g * rows + r, width)


def flat(panel):
    if isinstance(panel, tuple):
        return jnp.concatenate([piece[c] for c in range(2) for piece in panel], axis=0)
    return panel[...].reshape(-1, panel.shape[2])


def spectra_body(n_mode, wanted, carried, own, other, *refs):
    count = len(wanted)
    blocks, (out, buffer, sems) = refs[:count], refs[-3:]
    parts, lines, _ = out.shape
    copies = fetch(n_mode, wanted, (own, other), buffer, sems)
    for g, here, there in row_tiles(own.shape[0]):
        if here.start == 0:
            for b in range(count):
                copies[g, b].wait()
        total = out[:, :, there].reshape(parts * lines, -1) if carried else None
        for b, panel in enumerate(blocks):
            term = nt(flat(panel), buffer[g, b, here, :])
            total = term if total is None else total + term
        out[:, :, there] = total.reshape(parts, lines, -1)


def add_spectra(n_mode, blocks, wanted, both, spectra):
    parts, lines, modes = blocks[0].shape
    count = len(blocks)
    operands, aliases = list(blocks), {}
    if spectra is not None:
        aliases = {count: 0}
        operands.append(pinned(spectra))
    body = functools.partial(spectra_body, n_mode, wanted, spectra is not None)
    shape = (parts, lines, 2 * both[0].shape[0])
    return on_chip(body, [(shape, F32)], operands, "add_spectra", both, count, modes, aliases)[0]


def cos_sin(phases):
    turn = (phases + HARM // 8) >> 10
    x = (phases - (turn << 10)).astype(F32) * (2.0 * math.pi / HARM)
    xx = x * x
    sine = x * (1.0 + xx * (-1 / 6 + xx * (1 / 120 + xx * (-1 / 5040 + xx * (1 / 362880)))))
    cosine = 1.0 + xx * (-1 / 2 + xx * (1 / 24 + xx * (-1 / 720 + xx * (1 / 40320 - xx / 3628800))))
    odd = (turn & 1) == 1
    turn = turn & 3
    first, second = jnp.where(odd, sine, cosine), jnp.where(odd, cosine, sine)
    minus_cos = (turn == 1) | (turn == 2)
    return jnp.where(minus_cos, -first, first), jnp.where(turn >= 2, -second, second)


def table_body(harmonic, table, weights):
    steps, lines = table.shape[0] // 2, table.shape[1] // 2
    total_lines = harmonic.shape[1] * 2
    core = lax.rem(lax.axis_index("mode"), 2)
    mine = harmonic[:, pl.ds(pl.multiple_of(core * lines, lines), lines)]
    ratios = mine.astype(F32) * (1.0 / HARM)
    squared = ratios * ratios
    ones = jnp.ones_like(ratios)
    rows = [ones, ratios, squared, squared * squared] * 2
    weights[...] = (jnp.concatenate(rows, axis=0) * (1.0 / total_lines)).T
    scale = math.sqrt(2.0 / total_lines)
    tile = 32

    def fill(i, _):
        here = pl.multiple_of(i * tile, tile)
        ids = lax.broadcasted_iota(jnp.int32, (tile, lines), 0) + here
        cosine, sine = cos_sin((ids * mine) & (HARM - 1))
        for at, value in ((0, scale * cosine), (lines, -scale * sine)):
            head, tail = kernel_split(value)
            table[pl.ds(here, tile), at : at + lines] = head
            table[pl.ds(steps + here, tile), at : at + lines] = tail
        return 0

    lax.fori_loop(0, steps // tile, fill, 0)


def weights_body(n_mode, wanted, own, other, *refs):
    pairs, (w, v, buffer, sems) = refs[:4], refs[4:]
    copies = fetch(n_mode, wanted, (own, other), buffer, sems)
    elems = pairs[0].shape[2]
    modes = buffer.shape[3]
    rows = own.shape[0]
    place = lax.axis_index("mode")
    bases = (place * rows, (place + 1 - 2 * lax.rem(place, 2)) * rows)
    slots = lax.broadcasted_iota(jnp.int32, (elems, rows), 1).astype(F32)
    for p, pair in enumerate(pairs):
        local, value = (pair[0] - bases[p // 2].astype(F32)).T, pair[1].T
        weight = jnp.zeros((elems, rows), F32)
        for k in range(local.shape[1]):
            weight += jnp.where(local[:, k : k + 1] == slots, value[:, k : k + 1], 0.0)
        head, tail = kernel_split(weight)
        w[p * elems : (p + 1) * elems, :] = head
        w[(4 + p) * elems : (5 + p) * elems, :] = tail
    for g in range(2):
        head_rows = slice(2 * g * elems, 2 * (g + 1) * elems)
        tail_rows = slice((4 + 2 * g) * elems, (6 + 2 * g) * elems)
        for b in range(len(wanted)):
            copies[g, b].wait()
            part = buffer[g, b]
            head, tail = kernel_split(nn(w[head_rows, :], part) + nn(w[tail_rows, :], part))
            v[head_rows, b * modes : (b + 1) * modes] = head
            v[tail_rows, b * modes : (b + 1) * modes] = tail


def stress_body(spectra, w, table, out):
    parts, lines, both = spectra.shape
    rows, elems = both // 2, out.shape[0] // 2
    steps = out.shape[1]
    for g in range(2):
        here = slice(g * elems, (g + 1) * elems)
        values = spectra[:, :, g * rows : (g + 1) * rows].reshape(parts * lines, rows)
        s_head, s_tail = kernel_split(values)
        w_head, w_tail = w[here, :], w[(2 + g) * elems : (3 + g) * elems, :]
        picked = nt(w_head, s_head) + nt(w_head, s_tail) + nt(w_tail, s_head)
        p_head, p_tail = kernel_split(picked)
        t_head = table[:steps]
        out[here, :] = nt(p_head, t_head) + nt(p_tail, t_head) + nt(p_head, table[steps:])


def time_term(panel, v, table):
    steps, elems = table.shape[0] // 2, v.shape[0] // 2
    grid = nn(table[...], panel)
    g_head, g_tail = kernel_split(grid[:steps] + grid[steps:])
    total = nt(v, g_head)
    return total[:elems] + total[elems:] + nt(v[:elems], g_tail)


def half_body(near, far, v, columns, table, spectra, stress, spectra_out, stress_out):
    parts, lines, _ = spectra.shape
    panel = flat((near, far))
    for g, here, there in row_tiles(columns.shape[2]):
        total = spectra[:, :, there].reshape(parts * lines, -1) + nt(panel, columns[g, 0, here, :])
        spectra_out[:, :, there] = total.reshape(parts, lines, -1)
    stress_out[...] = stress[...] + time_term(panel, v[:, : panel.shape[1]], table)


def last_body(near, far, v, table, before, keep, give):
    panel = flat((near, far))
    total = before[...] + time_term(panel, v[:, panel.shape[1] :], table)
    half = total.shape[0] // 2
    keep[...] = total[:half]
    give[...] = total[half:]


def moment_body(near, far, columns, spectra, weights, keep, give):
    parts, lines, _ = spectra.shape
    panel = flat((near, far))
    for g, here, there in row_tiles(columns.shape[2]):
        total = spectra[:, :, there].reshape(parts * lines, -1) + nt(panel, columns[g, 1, here, :])
        total = total * total
        power = total[:lines] + total[lines:]
        sums = [jnp.sum(power * weights[:, k : k + 1], axis=0, keepdims=True) for k in range(4)]
        (give if g else keep)[:, here] = jnp.concatenate(sums + sums, axis=0)


def paired_shards(n_mode, panels, shapes, harmonic, connect, recovery, *, steps):
    tie = lax.optimization_barrier
    core = lax.axis_index("mode") % 2
    layers = n_mode // 4
    ring = lambda a: lax.ppermute(a, "mode", [(i, (i + 4) % n_mode) for i in range(n_mode)])
    across = lambda a: lax.ppermute(a, "mode", [(i, i ^ 2) for i in range(n_mode)])
    mate = lambda a: lax.ppermute(a, "mode", [(i, i ^ 1) for i in range(n_mode)])
    peer = lambda a: lax.ppermute(a, "node", [(0, 1), (1, 0)])

    parts, both_lines, modes = panels.shape
    lines = both_lines // 2
    rows = shapes.shape[0]
    elems = connect.shape[0]

    mine = lax.dynamic_slice(panels, (0, core * lines, 0), (parts, lines, modes))
    theirs = lax.dynamic_slice(panels, (0, (1 - core) * lines, 0), (parts, lines, modes))
    z = [[mine], [mate(theirs)]]
    x = [[], []]
    both = (shapes, mate(shapes))
    out = [((2 * steps, 2 * lines), BF16), ((lines, 8), F32)]
    table, weights = on_chip(table_body, out, [harmonic.reshape(1, -1)], "table", flops=5 * 10**9)
    z[1][0], table, weights = tie((z[1][0], table, weights))

    spectra = None
    for s in range(layers - 1):
        for h in range(2):
            swapped = across(z[h][-1])
            moved = ring(z[h][-1])
            if s == 0 and h == 0:
                moved, swapped = tie((moved, swapped))
                blocks, wanted = [z[0][0], z[1][0]], [(0, 0, 0), (0, 0, 1)]
                spectra = add_spectra(n_mode, blocks, wanted, both, None)
            elif s == 1 and h == 0:
                moved, swapped, spectra, connect, recovery = tie(
                    (moved, swapped, spectra, connect, recovery)
                )
                packed = jnp.stack([connect.astype(F32).T, recovery.T])
                pairs = [packed, peer(packed), mate(packed)]
                pairs.append(mate(pairs[1]))
            elif s == 1 and h == 1:
                moved, swapped, spectra, pairs = tie((moved, swapped, spectra, pairs))
                out = [((8 * elems, rows), BF16), ((8 * elems, 2 * modes), BF16)]
                out.append(((2, 2, rows, modes), BF16))
                wanted = [(layers - 1, 1, 0), (layers - 1, 1, 1)]
                body = functools.partial(weights_body, n_mode, wanted)
                w, v, columns = on_chip(
                    body, out, pairs, "weights", both, 2, modes, keep_columns=True
                )
            elif s == 2 and h == 0:
                moved, swapped, spectra, w, v, columns = tie((moved, swapped, spectra, w, v, columns))
            else:
                moved, swapped, spectra = tie((moved, swapped, spectra))
            z[h].append(moved)
            x[h].append(swapped)
            wanted = [(s, 1, h), (s + 1, 0, h)]
            spectra = add_spectra(n_mode, [swapped, moved], wanted, both, spectra)
    cut = lines * 18 // 32
    ends = [(across(z[h][-1][:, :cut]), ring(x[h][-1][:, cut:])) for h in range(2)]
    w, v, columns, table = [pinned(a) for a in (w, v, columns, table)]
    out = [((4 * elems, steps), F32)]
    (stress,) = on_chip(stress_body, out, [pinned(spectra), w, table], "first_stress")
    ends[0], stress, spectra = tie((ends[0], stress, spectra))
    out.insert(0, (spectra.shape, F32))
    operands = [*ends[0], v, columns, table, pinned(spectra), pinned(stress)]
    spectra, stress = on_chip(half_body, out, operands, "half_stress", aliases={5: 0, 6: 1}, flops=5 * 10**9)
    ends[1], stress, spectra = tie((ends[1], stress, spectra))
    out = [((2 * elems, steps), F32)] * 2
    keep, give = on_chip(last_body, out, [*ends[1], v, table, pinned(stress)], "last_stress")
    give, spectra = tie((give, spectra))
    got = mate(give)
    out = [((8, rows), F32)] * 2
    operands = [*ends[1], columns, pinned(spectra), pinned(weights)]
    keep_m, give_m = on_chip(moment_body, out, operands, "moments")
    send = (keep[elems:] + got[elems:]).astype(BF16)
    half = keep_m + mate(give_m)
    stress = (keep[:elems] + got[:elems]) + peer(send).astype(F32)
    moments = half + peer(half)
    start = lax.axis_index("node") * (rows // 2)
    return stress, lax.dynamic_slice(moments, (0, start), (4, rows // 2))


def plain_shards(panels, shapes, harmonic, connect, recovery, *, steps, total_lines):
    highest = lax.Precision.HIGHEST
    rows_mode = shapes.shape[0]
    spectra = jnp.einsum(
        "cfm,rm->cfr",
        lax.all_gather(panels, "mode", axis=2, tiled=True),
        shapes,
        preferred_element_type=F32,
    )
    step_ids = jnp.arange(steps, dtype=jnp.int32)
    phases = harmonic[:, None] * step_ids[None, :] % HARM
    angles = phases.astype(F32) * (2.0 * math.pi / HARM)
    weights = moment_weights(harmonic, total_lines)
    history = jnp.einsum("fr,ft->rt", spectra[0], jnp.cos(angles), precision=highest)
    history = history - jnp.einsum("fr,ft->rt", spectra[1], jnp.sin(angles), precision=highest)
    power = spectra[0] * spectra[0] + spectra[1] * spectra[1]
    history = math.sqrt(2.0 / total_lines) * history
    moments = jnp.dot(weights, power, precision=highest)
    history = lax.psum_scatter(history, "node", scatter_dimension=0, tiled=True)
    moments = lax.psum_scatter(moments, "node", scatter_dimension=1, tiled=True)
    rows_in = lax.all_gather(history.astype(BF16), "node", axis=0, tiled=True)
    local = connect - lax.axis_index("mode") * rows_mode
    slots = jnp.arange(rows_mode, dtype=jnp.int32)
    hit = local[:, :, None] == slots[None, None, :]
    weight = jnp.sum(jnp.where(hit, recovery[:, :, None], 0.0), axis=1)
    stress = jnp.dot(weight, rows_in, preferred_element_type=F32, precision=highest)
    return stress, moments


STEPS = 512


def solution(mesh):
    n_mode, n_node = mesh.shape["mode"], mesh.shape["node"]

    def shards(panels, *rest):
        if n_node == 2 and n_mode % 4 == 0 and n_mode >= 8:
            return paired_shards(n_mode, panels, *rest, steps=STEPS)
        return plain_shards(panels, *rest, steps=STEPS, total_lines=panels.shape[1] * n_node)

    return jax.shard_map(
        shards,
        mesh=mesh,
        in_specs=(
            P(None, "node", "mode"),
            P("mode", None),
            P("node"),
            P(("mode", "node"), None),
            P(("mode", "node"), None),
        ),
        out_specs=(P(("mode", "node"), None), P(None, ("mode", "node"))),
        check_vma=False,
    )
```

```python
import functools
import math

import jax
import jax.numpy as jnp
from jax import lax
from jax.experimental import pallas as pl
from jax.experimental.pallas import tpu as pltpu
from jax.sharding import PartitionSpec as P

HARM = 4096
F32 = jnp.float32
BF16 = jnp.bfloat16


def moment_weights(harmonic, lines):
    ratios = harmonic.astype(F32) / HARM
    squared = ratios * ratios
    return jnp.stack([jnp.ones_like(ratios), ratios, squared, squared * squared]) / lines


def nt(a, b):
    return lax.dot_general(a, b, (((1,), (1,)), ((), ())), preferred_element_type=F32)


def nn(a, b):
    return jnp.dot(a, b, preferred_element_type=F32)


def kernel_split(value):
    head = value.astype(BF16)
    return head, (value - head.astype(F32)).astype(BF16)


VMEM = pl.BlockSpec(memory_space=pltpu.VMEM)
HBM = pl.BlockSpec(memory_space=pltpu.HBM)


def on_chip(
    body, out_shapes, operands, name, both=(), columns=0, modes=0, aliases=None, keep_columns=False, flops=1000
):
    outs = [pltpu.VMEM(shape, dtype) for shape, dtype in out_shapes]
    scratch = []
    if both:
        rows = both[0].shape[0]
        scratch = [pltpu.SemaphoreType.DMA((2, columns))]
        if not keep_columns:
            scratch.insert(0, pltpu.VMEM((2, columns, rows, modes), BF16))
    aliases = {len(both) + i: o for i, o in (aliases or {}).items()}
    return pl.pallas_call(
        body,
        out_shape=outs,
        in_specs=[HBM] * len(both) + [VMEM] * len(operands),
        out_specs=[VMEM] * len(outs),
        scratch_shapes=scratch,
        input_output_aliases=aliases,
        compiler_params=pltpu.CompilerParams(vmem_limit_bytes=16 << 20),
        cost_estimate=pl.CostEstimate(flops=flops, bytes_accessed=1000, transcendentals=0),
        name=name,
    )(*both, *operands)


def pinned(value):
    return pltpu.with_memory_space_constraint(value, pltpu.VMEM)


def ring_layer(at, layers):
    return jnp.where(2 * at < layers, 2 * at, 2 * (layers - at) - 1)


def ring_place(layer, layers):
    return jnp.where(layer % 2 == 0, layer // 2, layers - (layer + 1) // 2)


def fetch(n_mode, wanted, both, buffer, sems):
    modes = buffer.shape[3]
    place = lax.axis_index("mode")
    layers = n_mode // 4
    layer, side, core = lax.div(place, 4), lax.rem(lax.div(place, 2), 2), lax.rem(place, 2)
    copies = {}
    for b, (back, flip, half) in enumerate(wanted):
        at = ring_layer(lax.rem(ring_place(layer, layers) + (layers - back), layers), layers) * 4
        at = at + lax.rem(side + flip, 2) * 2 + lax.rem(core + half, 2)
        at = pl.ds(pl.multiple_of(at * modes, modes), modes)
        for g, table in enumerate(both):
            copies[g, b] = pltpu.make_async_copy(table.at[:, at], buffer.at[g, b], sems.at[g, b])
    for copy in copies.values():
        copy.start()
    return copies


def row_tiles(rows):
    width = min(rows, 256)
    for g in range(2):
        for r in range(0, rows, width):
            yield g, pl.ds(r, width), pl.ds(g * rows + r, width)


def flat(panel):
    if isinstance(panel, tuple):
        return jnp.concatenate([piece[c] for c in range(2) for piece in panel], axis=0)
    return panel[...].reshape(-1, panel.shape[2])


def spectra_body(n_mode, wanted, carried, own, other, *refs):
    count = len(wanted)
    blocks, (out, buffer, sems) = refs[:count], refs[-3:]
    parts, lines, _ = out.shape
    copies = fetch(n_mode, wanted, (own, other), buffer, sems)
    for g, here, there in row_tiles(own.shape[0]):
        if here.start == 0:
            for b in range(count):
                copies[g, b].wait()
        total = out[:, :, there].reshape(parts * lines, -1) if carried else None
        for b, panel in enumerate(blocks):
            term = nt(flat(panel), buffer[g, b, here, :])
            total = term if total is None else total + term
        out[:, :, there] = total.reshape(parts, lines, -1)


def add_spectra(n_mode, blocks, wanted, both, spectra):
    parts, lines, modes = blocks[0].shape
    count = len(blocks)
    operands, aliases = list(blocks), {}
    if spectra is not None:
        aliases = {count: 0}
        operands.append(pinned(spectra))
    body = functools.partial(spectra_body, n_mode, wanted, spectra is not None)
    shape = (parts, lines, 2 * both[0].shape[0])
    return on_chip(body, [(shape, F32)], operands, "add_spectra", both, count, modes, aliases)[0]


def cos_sin(phases):
    turn = (phases + HARM // 8) >> 10
    x = (phases - (turn << 10)).astype(F32) * (2.0 * math.pi / HARM)
    xx = x * x
    sine = x * (1.0 + xx * (-1 / 6 + xx * (1 / 120 + xx * (-1 / 5040 + xx * (1 / 362880)))))
    cosine = 1.0 + xx * (-1 / 2 + xx * (1 / 24 + xx * (-1 / 720 + xx * (1 / 40320 - xx / 3628800))))
    odd = (turn & 1) == 1
    turn = turn & 3
    first, second = jnp.where(odd, sine, cosine), jnp.where(odd, cosine, sine)
    minus_cos = (turn == 1) | (turn == 2)
    return jnp.where(minus_cos, -first, first), jnp.where(turn >= 2, -second, second)


def table_body(harmonic, table, weights):
    steps, lines = table.shape[0] // 2, table.shape[1] // 2
    total_lines = harmonic.shape[1] * 2
    core = lax.rem(lax.axis_index("mode"), 2)
    mine = harmonic[:, pl.ds(pl.multiple_of(core * lines, lines), lines)]
    ratios = mine.astype(F32) * (1.0 / HARM)
    squared = ratios * ratios
    ones = jnp.ones_like(ratios)
    rows = [ones, ratios, squared, squared * squared] * 2
    weights[...] = (jnp.concatenate(rows, axis=0) * (1.0 / total_lines)).T
    scale = math.sqrt(2.0 / total_lines)
    tile = 32

    def fill(i, _):
        here = pl.multiple_of(i * tile, tile)
        ids = lax.broadcasted_iota(jnp.int32, (tile, lines), 0) + here
        cosine, sine = cos_sin((ids * mine) & (HARM - 1))
        for at, value in ((0, scale * cosine), (lines, -scale * sine)):
            head, tail = kernel_split(value)
            table[pl.ds(here, tile), at : at + lines] = head
            table[pl.ds(steps + here, tile), at : at + lines] = tail
        return 0

    lax.fori_loop(0, steps // tile, fill, 0)


def weights_body(n_mode, wanted, own, other, *refs):
    pairs, (w, v, buffer, sems) = refs[:4], refs[4:]
    copies = fetch(n_mode, wanted, (own, other), buffer, sems)
    elems = pairs[0].shape[2]
    rows = own.shape[0]
    place = lax.axis_index("mode")
    bases = (place * rows, (place + 1 - 2 * lax.rem(place, 2)) * rows)
    slots = lax.broadcasted_iota(jnp.int32, (elems, rows), 1).astype(F32)
    for p, pair in enumerate(pairs):
        local, value = (pair[0] - bases[p // 2].astype(F32)).T, pair[1].T
        weight = jnp.zeros((elems, rows), F32)
        for k in range(local.shape[1]):
            weight += jnp.where(local[:, k : k + 1] == slots, value[:, k : k + 1], 0.0)
        head, tail = kernel_split(weight)
        w[p * elems : (p + 1) * elems, :] = head
        w[(4 + p) * elems : (5 + p) * elems, :] = tail
    for g in range(2):
        head_rows = slice(2 * g * elems, 2 * (g + 1) * elems)
        tail_rows = slice((4 + 2 * g) * elems, (6 + 2 * g) * elems)
        for b in range(len(wanted)):
            copies[g, b].wait()
        part = buffer[g, len(wanted) - 1]
        head, tail = kernel_split(nn(w[head_rows, :], part) + nn(w[tail_rows, :], part))
        v[head_rows, :] = head
        v[tail_rows, :] = tail


def stress_body(near, far, columns, spectra, w, table, spectra_out, out):
    parts, lines, both = spectra.shape
    rows, elems = both // 2, out.shape[0] // 2
    steps = out.shape[1]
    panel = flat((near, far))
    for g, here, there in row_tiles(rows):
        total = spectra[:, :, there].reshape(parts * lines, -1) + nt(panel, columns[g, 0, here, :])
        spectra_out[:, :, there] = total.reshape(parts, lines, -1)
    for g in range(2):
        here = slice(g * elems, (g + 1) * elems)
        values = spectra_out[:, :, g * rows : (g + 1) * rows].reshape(parts * lines, rows)
        s_head, s_tail = kernel_split(values)
        w_head, w_tail = w[here, :], w[(2 + g) * elems : (3 + g) * elems, :]
        picked = nt(w_head, s_head) + nt(w_head, s_tail) + nt(w_tail, s_head)
        p_head, p_tail = kernel_split(picked)
        t_head = table[:steps]
        out[here, :] = nt(p_head, t_head) + nt(p_tail, t_head) + nt(p_head, table[steps:])


def time_term(panel, v, table):
    steps, elems = table.shape[0] // 2, v.shape[0] // 2
    grid = nn(table[...], panel)
    g_head, g_tail = kernel_split(grid[:steps] + grid[steps:])
    total = nt(v, g_head)
    return total[:elems] + total[elems:] + nt(v[:elems], g_tail)


def last_body(near, far, v, table, before, keep, give):
    panel = flat((near, far))
    total = before[...] + time_term(panel, v[...], table)
    half = total.shape[0] // 2
    keep[...] = total[:half]
    give[...] = total[half:]


def moment_body(near, far, columns, spectra, weights, keep, give):
    parts, lines, _ = spectra.shape
    panel = flat((near, far))
    for g, here, there in row_tiles(columns.shape[2]):
        total = spectra[:, :, there].reshape(parts * lines, -1) + nt(panel, columns[g, 1, here, :])
        total = total * total
        power = total[:lines] + total[lines:]
        sums = [jnp.sum(power * weights[:, k : k + 1], axis=0, keepdims=True) for k in range(4)]
        (give if g else keep)[:, here] = jnp.concatenate(sums + sums, axis=0)


def paired_shards(n_mode, panels, shapes, harmonic, connect, recovery, *, steps):
    tie = lax.optimization_barrier
    core = lax.axis_index("mode") % 2
    layers = n_mode // 4
    order = [*range(0, layers, 2), *reversed(range(1, layers, 2))]
    after = {layer: order[(i + 1) % layers] for i, layer in enumerate(order)}
    ring = lambda a: lax.ppermute(a, "mode", [(i, after[i // 4] * 4 + i % 4) for i in range(n_mode)])
    across = lambda a: lax.ppermute(a, "mode", [(i, i ^ 2) for i in range(n_mode)])
    mate = lambda a: lax.ppermute(a, "mode", [(i, i ^ 1) for i in range(n_mode)])
    peer = lambda a: lax.ppermute(a, "node", [(0, 1), (1, 0)])

    parts, both_lines, modes = panels.shape
    lines = both_lines // 2
    rows = shapes.shape[0]
    elems = connect.shape[0]

    mine = lax.dynamic_slice(panels, (0, core * lines, 0), (parts, lines, modes))
    theirs = lax.dynamic_slice(panels, (0, (1 - core) * lines, 0), (parts, lines, modes))
    z = [[mine], [mate(theirs)]]
    x = [[], []]
    both = (shapes, mate(shapes))
    out = [((2 * steps, 2 * lines), BF16), ((lines, 8), F32)]
    table, weights = on_chip(table_body, out, [harmonic.reshape(1, -1)], "table", flops=10**11)
    z[1][0], table, weights = tie((z[1][0], table, weights))

    spectra = None
    for s in range(layers - 1):
        for h in range(2):
            swapped = across(z[h][-1])
            moved = ring(z[h][-1])
            if s == 0 and h == 0:
                moved, swapped = tie((moved, swapped))
                blocks, wanted = [z[0][0], z[1][0]], [(0, 0, 0), (0, 0, 1)]
                spectra = add_spectra(n_mode, blocks, wanted, both, None)
            elif s == 1 and h == 0:
                moved, swapped, spectra, connect, recovery = tie(
                    (moved, swapped, spectra, connect, recovery)
                )
                packed = jnp.stack([connect.astype(F32).T, recovery.T])
                pairs = [packed, peer(packed), mate(packed)]
                pairs.append(mate(pairs[1]))
            elif s == 1 and h == 1:
                moved, swapped, spectra, pairs = tie((moved, swapped, spectra, pairs))
                out = [((8 * elems, rows), BF16), ((8 * elems, modes), BF16)]
                out.append(((2, 2, rows, modes), BF16))
                wanted = [(layers - 1, 1, 0), (layers - 1, 1, 1)]
                body = functools.partial(weights_body, n_mode, wanted)
                w, v, columns = on_chip(
                    body, out, pairs, "weights", both, 2, modes, keep_columns=True
                )
            elif s == 2 and h == 0:
                moved, swapped, spectra, w, v, columns = tie((moved, swapped, spectra, w, v, columns))
            else:
                moved, swapped, spectra = tie((moved, swapped, spectra))
            z[h].append(moved)
            x[h].append(swapped)
            wanted = [(s, 1, h), (s + 1, 0, h)]
            spectra = add_spectra(n_mode, [swapped, moved], wanted, both, spectra)
    cut = lines // 2
    ends = [(across(z[h][-1][:, :cut]), ring(x[h][-1][:, cut:])) for h in range(2)]
    w, v, columns, table = [pinned(a) for a in (w, v, columns, table)]
    ends[0], spectra = tie((ends[0], spectra))
    out = [(spectra.shape, F32), ((4 * elems, steps), F32)]
    operands = [*ends[0], columns, pinned(spectra), w, table]
    spectra, stress = on_chip(
        stress_body, out, operands, "first_stress", aliases={3: 0}, flops=5 * 10**9
    )
    ends[1], stress, spectra = tie((ends[1], stress, spectra))
    out = [((2 * elems, steps), F32)] * 2
    keep, give = on_chip(last_body, out, [*ends[1], v, table, pinned(stress)], "last_stress")
    give, spectra = tie((give, spectra))
    got = mate(give)
    out = [((8, rows), F32)] * 2
    operands = [*ends[1], columns, pinned(spectra), pinned(weights)]
    keep_m, give_m = on_chip(moment_body, out, operands, "moments")
    send = (keep[elems:] + got[elems:]).astype(BF16)
    half = keep_m + mate(give_m)
    stress = (keep[:elems] + got[:elems]) + peer(send).astype(F32)
    moments = half + peer(half)
    start = lax.axis_index("node") * (rows // 2)
    return stress, lax.dynamic_slice(moments, (0, start), (4, rows // 2))


def plain_shards(panels, shapes, harmonic, connect, recovery, *, steps, total_lines):
    highest = lax.Precision.HIGHEST
    rows_mode = shapes.shape[0]
    spectra = jnp.einsum(
        "cfm,rm->cfr",
        lax.all_gather(panels, "mode", axis=2, tiled=True),
        shapes,
        preferred_element_type=F32,
    )
    step_ids = jnp.arange(steps, dtype=jnp.int32)
    phases = harmonic[:, None] * step_ids[None, :] % HARM
    angles = phases.astype(F32) * (2.0 * math.pi / HARM)
    weights = moment_weights(harmonic, total_lines)
    history = jnp.einsum("fr,ft->rt", spectra[0], jnp.cos(angles), precision=highest)
    history = history - jnp.einsum("fr,ft->rt", spectra[1], jnp.sin(angles), precision=highest)
    power = spectra[0] * spectra[0] + spectra[1] * spectra[1]
    history = math.sqrt(2.0 / total_lines) * history
    moments = jnp.dot(weights, power, precision=highest)
    history = lax.psum_scatter(history, "node", scatter_dimension=0, tiled=True)
    moments = lax.psum_scatter(moments, "node", scatter_dimension=1, tiled=True)
    rows_in = lax.all_gather(history.astype(BF16), "node", axis=0, tiled=True)
    local = connect - lax.axis_index("mode") * rows_mode
    slots = jnp.arange(rows_mode, dtype=jnp.int32)
    hit = local[:, :, None] == slots[None, None, :]
    weight = jnp.sum(jnp.where(hit, recovery[:, :, None], 0.0), axis=1)
    stress = jnp.dot(weight, rows_in, preferred_element_type=F32, precision=highest)
    return stress, moments


STEPS = 512


def solution(mesh):
    n_mode, n_node = mesh.shape["mode"], mesh.shape["node"]

    def shards(panels, *rest):
        if n_node == 2 and n_mode % 4 == 0 and n_mode >= 8:
            return paired_shards(n_mode, panels, *rest, steps=STEPS)
        return plain_shards(panels, *rest, steps=STEPS, total_lines=panels.shape[1] * n_node)

    return jax.shard_map(
        shards,
        mesh=mesh,
        in_specs=(
            P(None, "node", "mode"),
            P("mode", None),
            P("node"),
            P(("mode", "node"), None),
            P(("mode", "node"), None),
        ),
        out_specs=(P(("mode", "node"), None), P(None, ("mode", "node"))),
        check_vma=False,
    )
```

```python
import functools
import math

import jax
import jax.numpy as jnp
from jax import lax
from jax.experimental import pallas as pl
from jax.experimental.pallas import tpu as pltpu
from jax.sharding import PartitionSpec as P

HARM = 4096
F32 = jnp.float32
BF16 = jnp.bfloat16


def moment_weights(harmonic, lines):
    ratios = harmonic.astype(F32) / HARM
    squared = ratios * ratios
    return jnp.stack([jnp.ones_like(ratios), ratios, squared, squared * squared]) / lines


def nt(a, b):
    return lax.dot_general(a, b, (((1,), (1,)), ((), ())), preferred_element_type=F32)


def nn(a, b):
    return jnp.dot(a, b, preferred_element_type=F32)


def kernel_split(value):
    head = value.astype(BF16)
    return head, (value - head.astype(F32)).astype(BF16)


VMEM = pl.BlockSpec(memory_space=pltpu.VMEM)
HBM = pl.BlockSpec(memory_space=pltpu.HBM)


def on_chip(
    body, out_shapes, operands, name, both=(), columns=0, modes=0, aliases=None, keep_columns=False, flops=1000
):
    outs = [pltpu.VMEM(shape, dtype) for shape, dtype in out_shapes]
    scratch = []
    if both:
        rows = both[0].shape[0]
        scratch = [pltpu.SemaphoreType.DMA((2, columns))]
        if not keep_columns:
            scratch.insert(0, pltpu.VMEM((2, columns, rows, modes), BF16))
    aliases = {len(both) + i: o for i, o in (aliases or {}).items()}
    return pl.pallas_call(
        body,
        out_shape=outs,
        in_specs=[HBM] * len(both) + [VMEM] * len(operands),
        out_specs=[VMEM] * len(outs),
        scratch_shapes=scratch,
        input_output_aliases=aliases,
        compiler_params=pltpu.CompilerParams(vmem_limit_bytes=16 << 20),
        cost_estimate=pl.CostEstimate(flops=flops, bytes_accessed=1000, transcendentals=0),
        name=name,
    )(*both, *operands)


def pinned(value):
    return pltpu.with_memory_space_constraint(value, pltpu.VMEM)


def ring_layer(at, layers):
    return jnp.where(2 * at < layers, 2 * at, 2 * (layers - at) - 1)


def ring_place(layer, layers):
    return jnp.where(layer % 2 == 0, layer // 2, layers - (layer + 1) // 2)


def fetch(n_mode, wanted, both, buffer, sems):
    modes = buffer.shape[3]
    place = lax.axis_index("mode")
    layers = n_mode // 4
    layer, side, core = lax.div(place, 4), lax.rem(lax.div(place, 2), 2), lax.rem(place, 2)
    copies = {}
    for b, (back, flip, half) in enumerate(wanted):
        at = ring_layer(lax.rem(ring_place(layer, layers) + (layers - back), layers), layers) * 4
        at = at + lax.rem(side + flip, 2) * 2 + lax.rem(core + half, 2)
        at = pl.ds(pl.multiple_of(at * modes, modes), modes)
        for g, table in enumerate(both):
            copies[g, b] = pltpu.make_async_copy(table.at[:, at], buffer.at[g, b], sems.at[g, b])
    for copy in copies.values():
        copy.start()
    return copies


def row_tiles(rows):
    width = min(rows, 256)
    for g in range(2):
        for r in range(0, rows, width):
            yield g, pl.ds(r, width), pl.ds(g * rows + r, width)


def flat(panel):
    if isinstance(panel, tuple):
        return jnp.concatenate([piece[c] for c in range(2) for piece in panel], axis=0)
    return panel[...].reshape(-1, panel.shape[2])


def spectra_body(n_mode, wanted, carried, own, other, *refs):
    count = len(wanted)
    blocks, (out, buffer, sems) = refs[:count], refs[-3:]
    parts, lines, _ = out.shape
    copies = fetch(n_mode, wanted, (own, other), buffer, sems)
    for g, here, there in row_tiles(own.shape[0]):
        if here.start == 0:
            for b in range(count):
                copies[g, b].wait()
        total = out[:, :, there].reshape(parts * lines, -1) if carried else None
        for b, panel in enumerate(blocks):
            term = nt(flat(panel), buffer[g, b, here, :])
            total = term if total is None else total + term
        out[:, :, there] = total.reshape(parts, lines, -1)


def add_spectra(n_mode, blocks, wanted, both, spectra):
    parts, lines, modes = blocks[0].shape
    count = len(blocks)
    operands, aliases = list(blocks), {}
    if spectra is not None:
        aliases = {count: 0}
        operands.append(pinned(spectra))
    body = functools.partial(spectra_body, n_mode, wanted, spectra is not None)
    shape = (parts, lines, 2 * both[0].shape[0])
    return on_chip(body, [(shape, F32)], operands, "add_spectra", both, count, modes, aliases)[0]


def cos_sin(phases):
    turn = (phases + HARM // 8) >> 10
    x = (phases - (turn << 10)).astype(F32) * (2.0 * math.pi / HARM)
    xx = x * x
    sine = x * (1.0 + xx * (-1 / 6 + xx * (1 / 120 + xx * (-1 / 5040 + xx * (1 / 362880)))))
    cosine = 1.0 + xx * (-1 / 2 + xx * (1 / 24 + xx * (-1 / 720 + xx * (1 / 40320 - xx / 3628800))))
    odd = (turn & 1) == 1
    turn = turn & 3
    first, second = jnp.where(odd, sine, cosine), jnp.where(odd, cosine, sine)
    minus_cos = (turn == 1) | (turn == 2)
    return jnp.where(minus_cos, -first, first), jnp.where(turn >= 2, -second, second)


def table_body(harmonic, table, weights):
    steps, lines = table.shape[0] // 2, table.shape[1] // 2
    total_lines = harmonic.shape[1] * 2
    core = lax.rem(lax.axis_index("mode"), 2)
    mine = harmonic[:, pl.ds(pl.multiple_of(core * lines, lines), lines)]
    ratios = mine.astype(F32) * (1.0 / HARM)
    squared = ratios * ratios
    ones = jnp.ones_like(ratios)
    rows = [ones, ratios, squared, squared * squared] * 2
    weights[...] = (jnp.concatenate(rows, axis=0) * (1.0 / total_lines)).T
    scale = math.sqrt(2.0 / total_lines)
    tile = 32

    def fill(i, _):
        here = pl.multiple_of(i * tile, tile)
        ids = lax.broadcasted_iota(jnp.int32, (tile, lines), 0) + here
        cosine, sine = cos_sin((ids * mine) & (HARM - 1))
        for at, value in ((0, scale * cosine), (lines, -scale * sine)):
            head, tail = kernel_split(value)
            table[pl.ds(here, tile), at : at + lines] = head
            table[pl.ds(steps + here, tile), at : at + lines] = tail
        return 0

    lax.fori_loop(0, steps // tile, fill, 0)


def weights_body(n_mode, wanted, own, other, *refs):
    pairs, (w, v, buffer, sems) = refs[:4], refs[4:]
    copies = fetch(n_mode, wanted, (own, other), buffer, sems)
    elems = pairs[0].shape[2]
    rows = own.shape[0]
    place = lax.axis_index("mode")
    bases = (place * rows, (place + 1 - 2 * lax.rem(place, 2)) * rows)
    slots = lax.broadcasted_iota(jnp.int32, (elems, rows), 1).astype(F32)
    for p, pair in enumerate(pairs):
        local, value = (pair[0] - bases[p // 2].astype(F32)).T, pair[1].T
        weight = jnp.zeros((elems, rows), F32)
        for k in range(local.shape[1]):
            weight += jnp.where(local[:, k : k + 1] == slots, value[:, k : k + 1], 0.0)
        head, tail = kernel_split(weight)
        w[p * elems : (p + 1) * elems, :] = head
        w[(4 + p) * elems : (5 + p) * elems, :] = tail
    for g in range(2):
        head_rows = slice(2 * g * elems, 2 * (g + 1) * elems)
        tail_rows = slice((4 + 2 * g) * elems, (6 + 2 * g) * elems)
        for b in range(len(wanted)):
            copies[g, b].wait()
        part = buffer[g, len(wanted) - 1]
        head, tail = kernel_split(nn(w[head_rows, :], part) + nn(w[tail_rows, :], part))
        v[head_rows, :] = head
        v[tail_rows, :] = tail


def stress_body(near, far, columns, spectra, w, table, spectra_out, out):
    parts, lines, both = spectra.shape
    rows, elems = both // 2, out.shape[0] // 2
    steps = out.shape[1]
    panel = flat((near, far))
    for g, here, there in row_tiles(rows):
        total = spectra[:, :, there].reshape(parts * lines, -1) + nt(panel, columns[g, 0, here, :])
        spectra_out[:, :, there] = total.reshape(parts, lines, -1)
    for g in range(2):
        here = slice(g * elems, (g + 1) * elems)
        values = spectra_out[:, :, g * rows : (g + 1) * rows].reshape(parts * lines, rows)
        s_head, s_tail = kernel_split(values)
        w_head, w_tail = w[here, :], w[(2 + g) * elems : (3 + g) * elems, :]
        picked = nt(w_head, s_head) + nt(w_head, s_tail) + nt(w_tail, s_head)
        p_head, p_tail = kernel_split(picked)
        t_head = table[:steps]
        out[here, :] = nt(p_head, t_head) + nt(p_tail, t_head) + nt(p_head, table[steps:])


def time_term(panel, v, table):
    steps, elems = table.shape[0] // 2, v.shape[0] // 2
    grid = nn(table[...], panel)
    g_head, g_tail = kernel_split(grid[:steps] + grid[steps:])
    total = nt(v, g_head)
    return total[:elems] + total[elems:] + nt(v[:elems], g_tail)


def last_body(near, far, v, table, before, keep, give):
    panel = flat((near, far))
    total = before[...] + time_term(panel, v[...], table)
    half = total.shape[0] // 2
    keep[...] = total[:half]
    give[...] = total[half:]


def moment_body(near, far, columns, spectra, weights, keep, give):
    parts, lines, _ = spectra.shape
    panel = flat((near, far))
    for g, here, there in row_tiles(columns.shape[2]):
        total = spectra[:, :, there].reshape(parts * lines, -1) + nt(panel, columns[g, 1, here, :])
        total = total * total
        power = total[:lines] + total[lines:]
        sums = [jnp.sum(power * weights[:, k : k + 1], axis=0, keepdims=True) for k in range(4)]
        (give if g else keep)[:, here] = jnp.concatenate(sums + sums, axis=0)


def paired_shards(n_mode, panels, shapes, harmonic, connect, recovery, *, steps):
    tie = lax.optimization_barrier
    core = lax.axis_index("mode") % 2
    layers = n_mode // 4
    order = [*range(0, layers, 2), *reversed(range(1, layers, 2))]
    after = {layer: order[(i + 1) % layers] for i, layer in enumerate(order)}
    ring = lambda a: lax.ppermute(a, "mode", [(i, after[i // 4] * 4 + i % 4) for i in range(n_mode)])
    across = lambda a: lax.ppermute(a, "mode", [(i, i ^ 2) for i in range(n_mode)])
    mate = lambda a: lax.ppermute(a, "mode", [(i, i ^ 1) for i in range(n_mode)])
    peer = lambda a: lax.ppermute(a, "node", [(0, 1), (1, 0)])

    parts, both_lines, modes = panels.shape
    lines = both_lines // 2
    rows = shapes.shape[0]
    elems = connect.shape[0]

    mine = lax.dynamic_slice(panels, (0, core * lines, 0), (parts, lines, modes))
    theirs = lax.dynamic_slice(panels, (0, (1 - core) * lines, 0), (parts, lines, modes))
    z = [[mine], [mate(theirs)]]
    x = [[], []]
    both = (shapes, mate(shapes))
    out = [((2 * steps, 2 * lines), BF16), ((lines, 8), F32)]
    table, weights = on_chip(table_body, out, [harmonic.reshape(1, -1)], "table", flops=10**11)
    z[1][0], table, weights = tie((z[1][0], table, weights))

    spectra = None
    for s in range(layers - 1):
        for h in range(2):
            swapped = across(z[h][-1])
            moved = ring(z[h][-1])
            if s == 0 and h == 0:
                moved, swapped = tie((moved, swapped))
                blocks, wanted = [z[0][0], z[1][0]], [(0, 0, 0), (0, 0, 1)]
                spectra = add_spectra(n_mode, blocks, wanted, both, None)
            elif s == 1 and h == 0:
                moved, swapped, spectra, connect, recovery = tie(
                    (moved, swapped, spectra, connect, recovery)
                )
                packed = jnp.stack([connect.astype(F32).T, recovery.T])
                pairs = [packed, peer(packed), mate(packed)]
                pairs.append(mate(pairs[1]))
            elif s == 1 and h == 1:
                moved, swapped, spectra, pairs = tie((moved, swapped, spectra, pairs))
                out = [((8 * elems, rows), BF16), ((8 * elems, modes), BF16)]
                out.append(((2, 2, rows, modes), BF16))
                wanted = [(layers - 1, 1, 0), (layers - 1, 1, 1)]
                body = functools.partial(weights_body, n_mode, wanted)
                w, v, columns = on_chip(
                    body, out, pairs, "weights", both, 2, modes, keep_columns=True
                )
            elif s == 2 and h == 0:
                moved, swapped, spectra, w, v, columns = tie((moved, swapped, spectra, w, v, columns))
            elif (s, h) == (layers - 2, 1):
                spectra = add_spectra(n_mode, [swapped], [(s, 1, h)], both, spectra)
                moved, swapped, spectra = tie((moved, swapped, spectra))
            else:
                moved, swapped, spectra = tie((moved, swapped, spectra))
            z[h].append(moved)
            x[h].append(swapped)
            if (s, h) == (layers - 2, 1):
                spectra = add_spectra(n_mode, [moved], [(s + 1, 0, h)], both, spectra)
            else:
                wanted = [(s, 1, h), (s + 1, 0, h)]
                spectra = add_spectra(n_mode, [swapped, moved], wanted, both, spectra)
    cut = lines // 2
    ends = [(across(z[h][-1][:, :cut]), ring(x[h][-1][:, cut:])) for h in range(2)]
    w, v, columns, table = [pinned(a) for a in (w, v, columns, table)]
    ends[0], spectra = tie((ends[0], spectra))
    out = [(spectra.shape, F32), ((4 * elems, steps), F32)]
    operands = [*ends[0], columns, pinned(spectra), w, table]
    spectra, stress = on_chip(
        stress_body, out, operands, "first_stress", aliases={3: 0}, flops=5 * 10**9
    )
    ends[1], stress, spectra = tie((ends[1], stress, spectra))
    out = [((2 * elems, steps), F32)] * 2
    keep, give = on_chip(last_body, out, [*ends[1], v, table, pinned(stress)], "last_stress")
    give, spectra = tie((give, spectra))
    got = mate(give)
    out = [((8, rows), F32)] * 2
    operands = [*ends[1], columns, pinned(spectra), pinned(weights)]
    keep_m, give_m = on_chip(moment_body, out, operands, "moments")
    got, keep_m, give_m = tie((got, keep_m, give_m))
    send = (keep[elems:] + got[elems:]).astype(BF16)
    half = keep_m + mate(give_m)
    stress = (keep[:elems] + got[:elems]) + peer(send).astype(F32)
    stress, other_half = tie((stress, peer(half)))
    moments = half + other_half
    start = lax.axis_index("node") * (rows // 2)
    return stress, lax.dynamic_slice(moments, (0, start), (4, rows // 2))


def plain_shards(panels, shapes, harmonic, connect, recovery, *, steps, total_lines):
    highest = lax.Precision.HIGHEST
    rows_mode = shapes.shape[0]
    spectra = jnp.einsum(
        "cfm,rm->cfr",
        lax.all_gather(panels, "mode", axis=2, tiled=True),
        shapes,
        preferred_element_type=F32,
    )
    step_ids = jnp.arange(steps, dtype=jnp.int32)
    phases = harmonic[:, None] * step_ids[None, :] % HARM
    angles = phases.astype(F32) * (2.0 * math.pi / HARM)
    weights = moment_weights(harmonic, total_lines)
    history = jnp.einsum("fr,ft->rt", spectra[0], jnp.cos(angles), precision=highest)
    history = history - jnp.einsum("fr,ft->rt", spectra[1], jnp.sin(angles), precision=highest)
    power = spectra[0] * spectra[0] + spectra[1] * spectra[1]
    history = math.sqrt(2.0 / total_lines) * history
    moments = jnp.dot(weights, power, precision=highest)
    history = lax.psum_scatter(history, "node", scatter_dimension=0, tiled=True)
    moments = lax.psum_scatter(moments, "node", scatter_dimension=1, tiled=True)
    rows_in = lax.all_gather(history.astype(BF16), "node", axis=0, tiled=True)
    local = connect - lax.axis_index("mode") * rows_mode
    slots = jnp.arange(rows_mode, dtype=jnp.int32)
    hit = local[:, :, None] == slots[None, None, :]
    weight = jnp.sum(jnp.where(hit, recovery[:, :, None], 0.0), axis=1)
    stress = jnp.dot(weight, rows_in, preferred_element_type=F32, precision=highest)
    return stress, moments


STEPS = 512


def solution(mesh):
    n_mode, n_node = mesh.shape["mode"], mesh.shape["node"]

    def shards(panels, *rest):
        if n_node == 2 and n_mode % 4 == 0 and n_mode >= 8:
            return paired_shards(n_mode, panels, *rest, steps=STEPS)
        return plain_shards(panels, *rest, steps=STEPS, total_lines=panels.shape[1] * n_node)

    return jax.shard_map(
        shards,
        mesh=mesh,
        in_specs=(
            P(None, "node", "mode"),
            P("mode", None),
            P("node"),
            P(("mode", "node"), None),
            P(("mode", "node"), None),
        ),
        out_specs=(P(("mode", "node"), None), P(None, ("mode", "node"))),
        check_vma=False,
    )
```
